768 devices in a mesh: lon: 192 (over x, y_hi, z, core), lat: 4 (over y_lo).
Axes of the slice: x: 4, y: 8 (y_hi: 2, y_lo: 4; y = y_hi * 4 + y_lo), z: 12, core: 2. Of those that a mesh axis runs over, the one named last changes fastest.
Arguments:
- thermal_anomaly: float32 [75, 384, 512], P(None, 'lon', 'lat'), may hold values from -6 to 6
- saltiness_anomaly: float32 [75, 384, 512], P(None, 'lon', 'lat'), may hold values from -6 to 6
- zonal_flow: float32 [75, 384, 512], P(None, 'lon', 'lat'), may hold values from -3 to 3
- meridional_flow: float32 [75, 384, 512], P(None, 'lon', 'lat'), may hold values from -3 to 3
- flooded_layer_number: int32 [384, 512], P('lon', 'lat'), may hold values from 0 to 75
- sideways_diffusion: float32 [384, 512], P('lon', 'lat'), may hold values from 0.2 to 4
- ambient_diffusion: float32 [384, 512], P('lon', 'lat'), may hold values from 0.1 to 10
Outputs:
- temp_next: float32 [75, 384, 512], P(None, 'lon', 'lat')
- salt_next: float32 [75, 384, 512], P(None, 'lon', 'lat')
- u_next: float32 [75, 384, 512], P(None, 'lon', 'lat')
- v_next: float32 [75, 384, 512], P(None, 'lon', 'lat')
The draws below stay inside these ranges and needn't reach their ends.
Inputs may be any that keep to these rules, and one draw needn't show every extreme that they name: flooded_layer_number counts wet levels from the top; 0 marks land.
All inputs are finite; a program needn't handle non-finite values.
Results may differ from the reference program's by a relative error of at most 0.0003.
Values sent between devices are 32-bit elements; how exact they have to be, the bound alone decides.
A program may use at most 64 MiB of HBM per device.

```python
import math
import jax
import jax.numpy as jnp

VERTICAL_LAYERS = 75
SUBSTEPS = 2
FOLD_OFFSET = 1
ZONAL_POINTS = 384
MERIDIAN_POINTS = 512


def with_ends(drawn, rng, smallest, top_value):
    shape = drawn.shape
    spot = [jax.random.randint(jax.random.fold_in(rng, axis), (), 0, shape[axis]) for axis in range(len(shape))]
    drawn = drawn.at[tuple(spot)].set(smallest)
    longest = shape.index(max(shape))
    spot[longest] = (spot[longest] + 1) % shape[longest]
    return drawn.at[tuple(spot)].set(top_value)


def shard_levels(key, extent, pieces, low, largest):
    level, own = 1.0, jax.random.fold_in(key, 6)
    for axis_at, parts in pieces:
        heights = jnp.exp(jax.random.uniform(jax.random.fold_in(own, axis_at), (parts,), jnp.float32, low / len(pieces), largest / len(pieces)))
        level = level * jnp.repeat(heights, extent[axis_at] // parts).reshape([-1 if axis == axis_at else 1 for axis in range(len(extent))])
    return level


def centred(rng, shape, deviation, reach, split=(), held_as=jnp.bfloat16):
    loudness = shard_levels(rng, shape, split, -0.22, 0.18) if split else 1.0
    values = jax.random.normal(rng, shape, jnp.float32) * deviation * loudness
    return jnp.minimum(jnp.maximum(values, -reach), reach).astype(held_as)


def setup_inputs(seed: int = 0) -> dict:
    keys = jax.random.split(jax.random.key(seed), 8)
    return {
        "thermal_anomaly": centred(keys[0], (VERTICAL_LAYERS, ZONAL_POINTS, MERIDIAN_POINTS), 1.0, 6.0, ((1, 192), (2, 4)), jnp.float32),
        "saltiness_anomaly": centred(keys[1], (VERTICAL_LAYERS, ZONAL_POINTS, MERIDIAN_POINTS), 1.0, 6.0, ((1, 192), (2, 4)), jnp.float32),
        "zonal_flow": centred(keys[2], (VERTICAL_LAYERS, ZONAL_POINTS, MERIDIAN_POINTS), 0.5, 3.0, ((1, 192), (2, 4)), jnp.float32),
        "meridional_flow": centred(keys[3], (VERTICAL_LAYERS, ZONAL_POINTS, MERIDIAN_POINTS), 0.5, 3.0, ((1, 192), (2, 4)), jnp.float32),
        "flooded_layer_number": with_ends(jax.random.randint(keys[4], (ZONAL_POINTS, MERIDIAN_POINTS), 0, VERTICAL_LAYERS + 1), jax.random.fold_in(keys[4], 1), 0, VERTICAL_LAYERS).astype(jnp.int32),
        "sideways_diffusion": jnp.clip(jnp.exp(math.log(4.0) - 2.9957323 * jax.random.uniform(keys[5], (ZONAL_POINTS, MERIDIAN_POINTS), jnp.float32) ** shard_levels(keys[5], (ZONAL_POINTS, MERIDIAN_POINTS), ((0, 192), (1, 4)), -0.2, 0.2)), 0.2, 4.0),
        "ambient_diffusion": jnp.clip(jnp.exp(math.log(10.0) - 4.6051702 * jax.random.uniform(keys[6], (ZONAL_POINTS, MERIDIAN_POINTS), jnp.float32) ** shard_levels(keys[6], (ZONAL_POINTS, MERIDIAN_POINTS), ((0, 192), (1, 4)), -0.2, 0.2)), 0.1, 10.0),
    }


dt_step = 0.05


def density(temp_field, salt_field):
    return 0.8 * salt_field - 0.2 * temp_field - 0.05 * temp_field * temp_field + 0.03 * temp_field * salt_field


def coriolis_rows(first_row, row_total, total_rows):
    row_index = first_row + jnp.arange(row_total, dtype=jnp.int32)
    mirrored = jnp.where(row_index >= total_rows, 2 * total_rows - 1 - row_index, row_index)
    return 0.2 + mirrored.astype(jnp.float32) / total_rows


def centre(array):
    return array[..., 1:-1, 1:-1]


def to_east(array):
    return array[..., 2:, 1:-1]


def to_west(array):
    return array[..., :-2, 1:-1]


def to_north(array):
    return array[..., 1:-1, 2:]


def to_south(array):
    return array[..., 1:-1, :-2]


def advance(padded, planet):
    layer_total = (padded.shape[0] - 2) // 4
    marine_state = padded[:4 * layer_total].reshape(4, layer_total, padded.shape[1], padded.shape[2])
    bottom = padded[4 * layer_total]
    lateral = padded[4 * layer_total + 1]
    level_index = jnp.arange(layer_total, dtype=jnp.float32)[:, None, None]
    wet_mask = (level_index < bottom[None]).astype(jnp.float32)
    pressure = 0.5 * jnp.cumsum(density(marine_state[0], marine_state[1]), axis=0)
    wet_centre = centre(wet_mask)
    lateral_centre = centre(lateral)
    field_centre = centre(marine_state)
    lateral_mix = jnp.zeros_like(field_centre)
    for neighbour in (to_east, to_west, to_north, to_south):
        face_coef = 0.5 * (lateral_centre + neighbour(lateral)) * wet_centre * neighbour(wet_mask)
        lateral_mix = lateral_mix + face_coef * (neighbour(marine_state) - field_centre)
    u_centre = field_centre[2]
    v_centre = field_centre[3]
    advection = u_centre * (to_east(marine_state) - to_west(marine_state)) * 0.5 + v_centre * (to_north(marine_state) - to_south(marine_state)) * 0.5
    tendency = lateral_mix - advection
    planet_rows = planet[1:-1]
    tend_u = tendency[2] + planet_rows * v_centre - (to_east(pressure) - to_west(pressure)) * 0.5
    tend_v = tendency[3] - planet_rows * u_centre - (to_north(pressure) - to_south(pressure)) * 0.5
    tendency = jnp.stack([tendency[0], tendency[1], tend_u, tend_v])
    updated = wet_centre * (field_centre + dt_step * tendency)
    return updated.reshape(4 * layer_total, updated.shape[2], updated.shape[3])


def vertical_mix(marine_state, wet_mask, ambient_diffusion):
    layer_total = marine_state.shape[1]
    density_now = density(marine_state[0], marine_state[1])
    stratification = density_now[1:] - density_now[:-1]
    coupling = ambient_diffusion[None] * (0.2 + 1.0 / (1.0 + 10.0 * jnp.maximum(stratification, 0.0))) * wet_mask[1:]
    zero_plane = jnp.zeros_like(ambient_diffusion)
    ratio_prev = zero_plane
    value_prev = jnp.zeros_like(marine_state[:, 0])
    ratio_list = []
    value_list = []
    for level in range(layer_total):
        lower_coef = coupling[level - 1] if level > 0 else zero_plane
        upper_coef = coupling[level] if level < layer_total - 1 else zero_plane
        pivot_value = 1.0 + lower_coef + upper_coef + lower_coef * ratio_prev
        ratio_prev = -upper_coef / pivot_value
        value_prev = (marine_state[:, level] + lower_coef * value_prev) / pivot_value
        ratio_list.append(ratio_prev)
        value_list.append(value_prev)
    current = value_list[layer_total - 1]
    solved = [current]
    for level in range(layer_total - 2, -1, -1):
        current = value_list[level] - ratio_list[level] * current
        solved.append(current)
    return jnp.stack(solved[::-1], axis=1)


def extend(combined, fold_signs, margin):
    lon_wrap = jnp.concatenate([combined[:, -margin:], combined, combined[:, :margin]], axis=1)
    mirror = jnp.roll(combined[:, ::-1, :], -FOLD_OFFSET, axis=1)
    mirror_wrap = jnp.concatenate([mirror[:, -margin:], mirror, mirror[:, :margin]], axis=1)
    folded = mirror_wrap[:, :, ::-1][:, :, :margin] * fold_signs[:, None, None]
    south_zero = jnp.zeros_like(lon_wrap[:, :, :margin])
    return jnp.concatenate([south_zero, lon_wrap, folded], axis=2)


def reference(thermal_anomaly, saltiness_anomaly, zonal_flow, meridional_flow, flooded_layer_number, sideways_diffusion, ambient_diffusion):
    layer_total = thermal_anomaly.shape[0]
    statics = jnp.stack([flooded_layer_number.astype(jnp.float32), sideways_diffusion])
    marine_state = jnp.concatenate([thermal_anomaly, saltiness_anomaly, zonal_flow, meridional_flow], axis=0)
    fold_signs = jnp.concatenate([jnp.ones((2 * layer_total,), jnp.float32), -jnp.ones((2 * layer_total,), jnp.float32), jnp.ones((2,), jnp.float32)])
    planet = coriolis_rows(-1, MERIDIAN_POINTS + 2, MERIDIAN_POINTS)
    for substep in range(SUBSTEPS):
        padded = extend(jnp.concatenate([marine_state, statics], axis=0), fold_signs, 1)
        marine_state = advance(padded, planet)
    level_index = jnp.arange(layer_total, dtype=jnp.float32)[:, None, None]
    wet_mask = (level_index < flooded_layer_number.astype(jnp.float32)[None]).astype(jnp.float32)
    final = vertical_mix(marine_state.reshape(4, layer_total, ZONAL_POINTS, MERIDIAN_POINTS), wet_mask, ambient_diffusion)
    return final[0], final[1], final[2], final[3]
```

```python
import functools

import jax
import jax.numpy as jnp
from jax import lax
from jax.experimental import pallas as pl
from jax.experimental.pallas import tpu as pltpu
from jax.sharding import PartitionSpec as P

MESH = pl.DeviceIdType.MESH
DT = 0.05
FIELDS = 4
COLUMNS = 2
SPAN = 128
LEVELS = 4
ROWS = LEVELS * COLUMNS
CHUNK = 4


def density(t, s):
    return s * (0.8 + 0.03 * t) - t * (0.2 + 0.05 * t)


def up(x, n):
    return pltpu.roll(x, n % ROWS, 0)


def along(x, n):
    return pltpu.roll(x, n % SPAN, 1)


def halo_and_levels(
    levels, lon_count, lat_count,
    t_in, s_in, u_in, v_in, flooded_in, lateral_in, ambient_in,
    y_out, r_out,
    own, east_tile, west_tile, flooded, lateral, ambient, pack, halo_n, halo_s, rim, rim_x, rim_new,
    local_sem, ew_send, ew_recv, static_send, static_recv, edge_send, edge_recv,
):
    fields_in = (t_in, s_in, u_in, v_in)
    groups = pl.cdiv(levels, LEVELS)
    me = lax.axis_index("lon")
    row = lax.axis_index("lat")
    east = lax.rem(me + 1, lon_count)
    west = lax.rem(me + lon_count - 1, lon_count)
    fold_a = lon_count - 1 - me
    fold_b = lax.rem(2 * lon_count - 2 - me, lon_count)
    top = row == lat_count - 1
    bottom = row == 0
    inner = jnp.logical_not(top)
    above = jnp.logical_not(bottom)
    b_other = jnp.logical_and(top, fold_b != me)
    b_self = jnp.logical_and(top, fold_b == me)
    north = row + 1
    south = row - 1

    barrier = pltpu.get_barrier_semaphore()

    def greet(lon, lat):
        pl.semaphore_signal(barrier, inc=1, device_id=(lon, lat), device_id_type=MESH)

    greet(east, row)
    greet(west, row)

    @pl.when(top)
    def _():
        greet(fold_a, row)

    @pl.when(b_other)
    def _():
        greet(fold_b, row)

    @pl.when(inner)
    def _():
        greet(me, north)
        greet(east, north)
        greet(west, north)

    @pl.when(above)
    def _():
        greet(me, south)
        greet(east, south)
        greet(west, south)

    flat = [x.reshape(levels * COLUMNS, SPAN) for x in fields_in]
    local = [
        pltpu.make_async_copy(flat[f], own.at[f, 0:levels * COLUMNS], local_sem.at[f])
        for f in range(FIELDS)
    ]
    local += [
        pltpu.make_async_copy(flooded_in, flooded.at[0], local_sem.at[4]),
        pltpu.make_async_copy(lateral_in, lateral.at[0], local_sem.at[5]),
        pltpu.make_async_copy(ambient_in, ambient, local_sem.at[6]),
    ]
    for copy in local:
        copy.start()
    for copy in local:
        copy.wait()

    lane = lax.broadcasted_iota(jnp.int32, (ROWS, SPAN), 1)
    sub = lax.broadcasted_iota(jnp.int32, (ROWS, SPAN), 0)
    quad = lane // 4
    place = lane % 4
    tier = sub // COLUMNS
    even = sub % COLUMNS == 0

    def tiled(x):
        return jnp.concatenate([x.astype(jnp.float32)] * LEVELS, axis=0)

    depth_own = tiled(flooded[0])
    mix_own = tiled(lateral[0])
    for f in range(FIELDS):
        def edges(g, acc):
            at = pl.multiple_of(g * ROWS, ROWS)
            return jnp.where(quad == g, pltpu.roll(own[f, pl.ds(at, ROWS)], 4 * g + 2, 1), acc)

        acc = lax.fori_loop(0, groups, edges, jnp.zeros((ROWS, SPAN), jnp.float32), unroll=True)
        if f == 0:
            acc = jnp.where(quad == groups, along(depth_own, 4 * groups + 2), acc)
            acc = jnp.where(quad == groups + 1, along(mix_own, 4 * groups + 6), acc)
        pack[f] = acc

    waits = (
        2 + 3 * inner.astype(jnp.int32) + 3 * above.astype(jnp.int32)
        + top.astype(jnp.int32) + b_other.astype(jnp.int32)
    )
    pl.semaphore_wait(barrier, waits)

    def edge(slot, lon, lat, sent):
        dst = halo_s if slot < 3 else halo_n
        return pltpu.make_async_remote_copy(
            src_ref=pack, dst_ref=dst.at[slot % 3],
            send_sem=edge_send.at[sent], recv_sem=edge_recv.at[slot],
            device_id=(lon, lat), device_id_type=MESH,
        )

    to_a = edge(3, fold_a, row, 6)
    to_b = edge(4, fold_b, row, 7)
    b_copy = pltpu.make_async_copy(pack, halo_n.at[1], local_sem.at[7])
    northward = (edge(0, me, north, 0), edge(1, west, north, 1), edge(2, east, north, 2))
    southward = (edge(3, me, south, 3), edge(4, west, south, 4), edge(5, east, south, 5))

    @pl.when(top)
    def _():
        to_a.start()

    @pl.when(b_other)
    def _():
        to_b.start()

    @pl.when(b_self)
    def _():
        b_copy.start()

    @pl.when(inner)
    def _():
        for copy in northward:
            copy.start()

    @pl.when(above)
    def _():
        for copy in southward:
            copy.start()

    sides = ((east, west_tile), (west, east_tile))
    statics = []
    for side, (lon, _) in enumerate(sides):
        for n, (src, dst) in enumerate(((flooded_in, flooded), (lateral_in, lateral))):
            statics.append(pltpu.make_async_remote_copy(
                src_ref=src, dst_ref=dst.at[1 + side],
                send_sem=static_send.at[side, n], recv_sem=static_recv.at[side, n],
                device_id=(lon, row), device_id_type=MESH,
            ))
    starts = list(range(0, groups, CHUNK))
    tiles = []
    for c, first in enumerate(starts):
        lo = first * ROWS
        hi = min((first + CHUNK) * ROWS, levels * COLUMNS)
        part = []
        for f in range(FIELDS):
            for side, (lon, dst) in enumerate(sides):
                part.append(pltpu.make_async_remote_copy(
                    src_ref=flat[f].at[lo:hi], dst_ref=dst.at[f, lo:hi],
                    send_sem=ew_send.at[side, c, f], recv_sem=ew_recv.at[side, c, f],
                    device_id=(lon, row), device_id_type=MESH,
                ))
        tiles.append(part)
    for copy in statics:
        copy.start()
    for part in tiles:
        for copy in part:
            copy.start()

    for copy in statics:
        copy.wait_recv()

    @pl.when(above)
    def _():
        for copy in northward:
            copy.wait_recv()

    @pl.when(inner)
    def _():
        for copy in southward:
            copy.wait_recv()

    @pl.when(top)
    def _():
        to_a.wait_recv()

    @pl.when(b_other)
    def _():
        to_b.wait_recv()

    @pl.when(b_self)
    def _():
        b_copy.wait()

    def sideways(o, x):
        return jnp.where(even, up(o, -1), up(x, 1)), jnp.where(even, up(x, -1), up(o, 1))

    def prefix(d):
        two = up(d, COLUMNS)
        s = d + jnp.where(tier >= 1, two, 0.0)
        pair = d + two
        return s + jnp.where(tier >= 2, up(s, 2 * COLUMNS), 0.0), pair + up(pair, 2 * COLUMNS)

    def packed_pressure(t, s):
        inside, total = prefix(0.5 * density(t, s))
        for n in (4, 8, 16, 32, 64):
            total = total + jnp.where(lane >= n, along(total, n), 0.0)
        return inside + jnp.where(lane >= 4, along(total, 4), 0.0)

    def every_quad(x, n):
        x = jnp.where(quad == n, x, 0.0)
        for n in (4, 8, 16, 32, 64):
            x = x + along(x, n)
        return x

    for f in range(FIELDS):
        sign = 1.0 if f < 2 else -1.0
        n0, n1, n2 = halo_n[0, f], halo_n[1, f], halo_n[2, f]
        s0, s1, s2 = halo_s[0, f], halo_s[1, f], halo_s[2, f]
        for dst, n, s, fold in (
            (rim, n0, s0, jnp.where(even, n0, n1)),
            (rim_x, jnp.where(even, n1, n2), jnp.where(even, s1, s2), jnp.where(even, n1, n0)),
        ):
            n = jnp.where(place == 1, along(n, -1), along(n, -3))
            n = jnp.where(top, sign * fold, n)
            s = jnp.where(place == 2, along(s, 1), along(s, 3))
            s = jnp.where(bottom, 0.0, s)
            dst[f] = jnp.where(place < 2, n, s)

    def turning(j):
        total = lat_count * SPAN
        m = jnp.where(j >= total, 2 * total - 1 - j, j)
        return DT * (0.2 + m.astype(jnp.float32) / total)

    def faces(depth, mix, sides_of):
        return [(jnp.minimum(depth, d), mix + m) for d, m in zip(sides_of(0), sides_of(1))]

    def weights(level, depth, around):
        c = [jnp.where(level < d, m, 0.0) for d, m in around]
        return c, 1.0 - ((c[0] + c[1]) + (c[2] + c[3])), level < depth

    def update(weight, turn, cells, e, w, n, s):
        (ce, cw, cn, cs), keep, wet = weight
        half_u = (0.5 * DT) * cells[2]
        half_v = (0.5 * DT) * cells[3]
        ce, cw, cn, cs = ce - half_u, cw + half_u, cn - half_v, cs + half_v
        out = []
        for f in range(FIELDS):
            x = (keep * cells[f] + ce * e[f]) + (cw * w[f] + (cn * n[f] + cs * s[f]))
            if f == 2:
                x = x + (turn * cells[3] - (0.5 * DT) * (e[4] - w[4]))
            if f == 3:
                x = x - (turn * cells[2] + (0.5 * DT) * (n[4] - s[4]))
            out.append(jnp.where(wet, x, 0.0))
        return out

    own_edge = [pack[f] for f in range(FIELDS)]
    cells = [rim[f] for f in range(FIELDS)]
    cells_x = [rim_x[f] for f in range(FIELDS)]
    rim_depth, rim_mix = every_quad(cells[0], groups), (0.5 * DT) * every_quad(cells[0], groups + 1)
    x_depth, x_mix = every_quad(cells_x[0], groups), (0.5 * DT) * every_quad(cells_x[0], groups + 1)
    o_depth, o_mix = every_quad(own_edge[0], groups), (0.5 * DT) * every_quad(own_edge[0], groups + 1)
    for block in (own_edge, cells, cells_x):
        block.append(packed_pressure(block[0], block[1]))
    rim[4] = cells[4]
    rim_x[4] = cells_x[4]

    def around_rim(c, x, o):
        e, w = sideways(c, x)
        return e, w, jnp.where(place == 1, along(c, 1), o), jnp.where(place == 2, along(c, -1), o)

    around = [around_rim(*q) for q in zip(cells, cells_x, own_edge)]
    statics_around = (around_rim(rim_depth, x_depth, o_depth), around_rim(rim_mix, x_mix, o_mix))
    rim_level = (LEVELS * quad + tier).astype(jnp.float32)
    rim_row = jnp.where(place < 2, (row + 1) * SPAN + 1 - place, row * SPAN + 1 - place)
    new = update(
        weights(rim_level, rim_depth, faces(rim_depth, rim_mix, lambda n: statics_around[n])),
        turning(rim_row), cells, *[[q[n] for q in around] for n in range(4)],
    )
    new.append(packed_pressure(new[0], new[1]))
    for q in range(FIELDS + 1):
        rim_new[q] = new[q]

    first_lane = lane == 0
    last_lane = lane == SPAN - 1

    def beside(x, r):
        return jnp.where(last_lane, r, along(x, -1)), jnp.where(first_lane, r, along(x, 1))

    def shifted(x, g):
        return pltpu.roll(x, lax.rem(2 * SPAN - 2 - 4 * g, SPAN) if not isinstance(g, int) else (-2 - 4 * g) % SPAN, 1)

    def around_own(o, x, r):
        return sideways(o, x) + beside(o, r)

    def around_x(o, x, z, r):
        return (jnp.where(even, z, up(o, 1)), jnp.where(even, up(o, -1), z)) + beside(x, r)

    def split(e, w):
        return jnp.where(even, e, w), jnp.where(even, up(e, -1), up(w, 1))

    depth_x, depth_z = split(tiled(flooded[2]), tiled(flooded[1]))
    mix_x, mix_z = split(tiled(lateral[2]), tiled(lateral[1]))
    mix_o, mix_x, mix_z = ((0.5 * DT) * x for x in (mix_own, mix_x, mix_z))
    rim_depth_at, rim_mix_at = shifted(rim_depth, 0), shifted(rim_mix, 0)
    x_depth_at, x_mix_at = shifted(x_depth, 0), shifted(x_mix, 0)
    own_statics = (around_own(depth_own, depth_x, rim_depth_at), around_own(mix_o, mix_x, rim_mix_at))
    x_statics = (
        around_x(depth_own, depth_x, depth_z, x_depth_at), around_x(mix_o, mix_x, mix_z, x_mix_at)
    )
    own_faces = faces(depth_own, mix_o, lambda n: own_statics[n])
    x_faces = faces(depth_x, mix_x, lambda n: x_statics[n])
    turn = turning(row * SPAN + lane)
    ambient_all = tiled(ambient[...])
    tier_level = tier.astype(jnp.float32)
    low = tier % 2 == 0
    lower_half = tier < 2

    def per_level(blocks):
        a, b, c, d = blocks
        ab0, ab1 = jnp.where(low, a, up(b, 2)), jnp.where(low, up(a, -2), b)
        cd0, cd1 = jnp.where(low, c, up(d, 2)), jnp.where(low, up(c, -2), d)
        return (
            jnp.where(lower_half, ab0, up(cd0, 4)), jnp.where(lower_half, ab1, up(cd1, 4)),
            jnp.where(lower_half, up(ab0, 4), cd0), jnp.where(lower_half, up(ab1, 4), cd1),
        )

    def repeated(a):
        ab0, ab1 = jnp.where(low, a, up(a, 2)), jnp.where(low, up(a, -2), a)
        r0, r1 = up(ab0, 4), up(ab1, 4)
        return (
            jnp.where(lower_half, ab0, r0), jnp.where(lower_half, ab1, r1),
            jnp.where(lower_half, r0, ab0), jnp.where(lower_half, r1, ab1),
        )

    def step(g, carry):
        po, px, pz, p2o, p2x, heavy, held, lower, inverse, value = carry
        at = pl.multiple_of(g * ROWS, ROWS)
        o = [own[f, pl.ds(at, ROWS)] for f in range(FIELDS)]
        xz = [split(east_tile[f, pl.ds(at, ROWS)], west_tile[f, pl.ds(at, ROWS)]) for f in range(FIELDS)]
        x, z = [q[0] for q in xz], [q[1] for q in xz]
        pressures = []
        for block, total in ((o, po), (x, px), (z, pz)):
            inside, more = prefix(0.5 * density(block[0], block[1]))
            block.append(inside + total)
            pressures.append(total + more)
        level = tier_level + (LEVELS * g).astype(jnp.float32)
        around = [around_own(*q, shifted(rim[n], g)) for n, q in enumerate(zip(o, x))]
        weight = weights(level, depth_own, own_faces)
        o2 = update(weight, turn, o, *[[q[n] for q in around] for n in range(4)])
        around = [around_x(*q, shifted(rim_x[n], g)) for n, q in enumerate(zip(o, x, z))]
        x2 = update(
            weights(level, depth_x, x_faces), turn, x, *[[q[n] for q in around] for n in range(4)]
        )
        for block, total in ((o2, p2o), (x2, p2x)):
            inside, more = prefix(0.5 * density(block[0], block[1]))
            block.append(inside + total)
            pressures.append(total + more)
        around = [around_own(*q, shifted(rim_new[n], g)) for n, q in enumerate(zip(o2, x2))]
        done = update(weight, turn, o2, *[[q[n] for q in around] for n in range(4)])

        new_heavy = up(density(done[0], done[1]), COLUMNS)
        rise = density(done[0], done[1]) - jnp.where(tier == 0, heavy, new_heavy)
        a = ambient_all * (0.2 + 1.0 / (1.0 + 10.0 * jnp.maximum(rise, 0.0)))
        a = jnp.where(jnp.logical_and(weight[2], level > 0.5), a, 0.0)
        uppers = repeated(a)
        fields = per_level(done)
        xs = (held,) + fields[:3]
        lowers = (lower,) + uppers[:3]
        dets = []
        last, before = None, inverse
        for n in range(LEVELS):
            main = 1.0 + (lowers[n] + uppers[n])
            square = lowers[n] * lowers[n]
            if n == 0:
                det = main - square * before
            elif n == 1:
                det = main * last - square
            else:
                det = main * last - square * before
            dets.append(det)
            last, before = det, last
        for n in range(LEVELS):
            inverse = 1.0 / dets[n]
            if n > 0:
                inverse = inverse * dets[n - 1]
            value = (xs[n] + lowers[n] * value) * inverse
            y_out[LEVELS * g + n] = value
            r_out[LEVELS * g + n] = uppers[n] * inverse
        return (*pressures, new_heavy, fields[3], uppers[3], inverse, value)

    zero = jnp.zeros((ROWS, SPAN), jnp.float32)
    carry = (zero,) * 8 + (zero + 1.0, zero)
    for c, first in enumerate(starts):
        for copy in tiles[c]:
            copy.wait_recv()
        carry = lax.fori_loop(first, min(first + CHUNK, groups), step, carry, unroll=2)

    for part in tiles:
        for copy in part:
            copy.wait_send()
    for copy in statics:
        copy.wait_send()

    @pl.when(top)
    def _():
        to_a.wait_send()

    @pl.when(b_other)
    def _():
        to_b.wait_send()

    @pl.when(inner)
    def _():
        for copy in northward:
            copy.wait_send()

    @pl.when(above)
    def _():
        for copy in southward:
            copy.wait_send()


def substitute(levels, y, r, t_out, s_out, u_out, v_out, result, sem):
    outs = (t_out, s_out, u_out, v_out)
    cuts = [0, levels // 3, 2 * levels // 3, levels]
    current = y[levels]
    result[levels - 1] = current
    copies = []
    for n in range(len(cuts) - 2, -1, -1):
        lo, hi = cuts[n], cuts[n + 1]
        for k in range(min(hi, levels - 1) - 1, lo - 1, -1):
            current = y[k + 1] + r[k + 1] * current
            result[k] = current
        for f in range(FIELDS):
            copies.append(pltpu.make_async_copy(
                result.at[lo:hi, COLUMNS * f:COLUMNS * (f + 1), :], outs[f].at[lo:hi], sem.at[n, f]
            ))
            copies[-1].start()
    for copy in copies:
        copy.wait()


def solution(mesh):
    lon_count, lat_count = mesh.shape["lon"], mesh.shape["lat"]

    def shards(*args):
        levels = args[0].shape[0]
        groups = pl.cdiv(levels, LEVELS)
        chunks = pl.cdiv(groups, CHUNK)
        f32 = jnp.float32
        vmem = pl.BlockSpec(memory_space=pltpu.VMEM)
        anywhere = pl.BlockSpec(memory_space=pl.ANY)
        y, r = pl.pallas_call(
            functools.partial(halo_and_levels, levels, lon_count, lat_count),
            out_shape=[jax.ShapeDtypeStruct((groups * LEVELS, ROWS, SPAN), f32)] * 2,
            in_specs=[anywhere] * 7,
            out_specs=[vmem] * 2,
            scratch_shapes=[
                pltpu.VMEM((FIELDS, groups * ROWS, SPAN), f32),
                pltpu.VMEM((FIELDS, groups * ROWS, SPAN), f32),
                pltpu.VMEM((FIELDS, groups * ROWS, SPAN), f32),
                pltpu.VMEM((3, COLUMNS, SPAN), jnp.int32),
                pltpu.VMEM((3, COLUMNS, SPAN), f32),
                pltpu.VMEM((COLUMNS, SPAN), f32),
                pltpu.VMEM((FIELDS, ROWS, SPAN), f32),
                pltpu.VMEM((3, FIELDS, ROWS, SPAN), f32),
                pltpu.VMEM((3, FIELDS, ROWS, SPAN), f32),
                pltpu.VMEM((FIELDS + 1, ROWS, SPAN), f32),
                pltpu.VMEM((FIELDS + 1, ROWS, SPAN), f32),
                pltpu.VMEM((FIELDS + 1, ROWS, SPAN), f32),
                pltpu.SemaphoreType.DMA((8,)),
                pltpu.SemaphoreType.DMA((2, chunks, FIELDS)),
                pltpu.SemaphoreType.DMA((2, chunks, FIELDS)),
                pltpu.SemaphoreType.DMA((2, 2)),
                pltpu.SemaphoreType.DMA((2, 2)),
                pltpu.SemaphoreType.DMA((8,)),
                pltpu.SemaphoreType.DMA((6,)),
            ],
            compiler_params=pltpu.CompilerParams(collective_id=0, has_side_effects=True),
        )(*args)
        return pl.pallas_call(
            functools.partial(substitute, levels),
            out_shape=[jax.ShapeDtypeStruct(args[0].shape, f32)] * FIELDS,
            in_specs=[vmem] * 2,
            out_specs=[anywhere] * FIELDS,
            scratch_shapes=[
                pltpu.VMEM((levels, ROWS, SPAN), f32),
                pltpu.SemaphoreType.DMA((3, FIELDS)),
            ],
        )(y, r)

    wide, flat = P(None, "lon", "lat"), P("lon", "lat")
    return jax.shard_map(
        shards,
        mesh=mesh,
        in_specs=(wide,) * 4 + (flat,) * 3,
        out_specs=(wide,) * 4,
        check_vma=False,
    )
```

```python
import functools

import jax
import jax.numpy as jnp
from jax import lax
from jax.experimental import pallas as pl
from jax.experimental.pallas import tpu as pltpu
from jax.sharding import PartitionSpec as P

MESH = pl.DeviceIdType.MESH
DT = 0.05
FIELDS = 4
COLUMNS = 2
SPAN = 128
LEVELS = 4
ROWS = LEVELS * COLUMNS


def cuts_of(groups):
    return [0, *range(3, groups - 1, 4), groups]


def density(t, s):
    return s * (0.8 + 0.03 * t) - t * (0.2 + 0.05 * t)


def up(x, n):
    return pltpu.roll(x, n % ROWS, 0)


def along(x, n):
    return pltpu.roll(x, n % SPAN, 1)


def halo_and_levels(
    levels, lon_count, lat_count,
    t_in, s_in, u_in, v_in, flooded_in, lateral_in, ambient_in,
    y_out, r_out,
    own, east_tile, west_tile, flooded, lateral, ambient, pack, halo_n, halo_s, rim, rim_x, rim_new,
    local_sem, ew_send, ew_recv, static_send, static_recv, edge_send, edge_recv,
):
    fields_in = (t_in, s_in, u_in, v_in)
    groups = pl.cdiv(levels, LEVELS)
    me = lax.axis_index("lon")
    row = lax.axis_index("lat")
    east = lax.rem(me + 1, lon_count)
    west = lax.rem(me + lon_count - 1, lon_count)
    fold_a = lon_count - 1 - me
    fold_b = lax.rem(2 * lon_count - 2 - me, lon_count)
    top = row == lat_count - 1
    bottom = row == 0
    inner = jnp.logical_not(top)
    above = jnp.logical_not(bottom)
    b_other = jnp.logical_and(top, fold_b != me)
    b_self = jnp.logical_and(top, fold_b == me)
    north = row + 1
    south = row - 1

    barrier = pltpu.get_barrier_semaphore()

    def greet(lon, lat):
        pl.semaphore_signal(barrier, inc=1, device_id=(lon, lat), device_id_type=MESH)

    greet(east, row)
    greet(west, row)

    @pl.when(top)
    def _():
        greet(fold_a, row)

    @pl.when(b_other)
    def _():
        greet(fold_b, row)

    @pl.when(inner)
    def _():
        greet(me, north)
        greet(east, north)
        greet(west, north)

    @pl.when(above)
    def _():
        greet(me, south)
        greet(east, south)
        greet(west, south)

    flat = [x.reshape(levels * COLUMNS, SPAN) for x in fields_in]
    local = [
        pltpu.make_async_copy(flat[f], own.at[f, 0:levels * COLUMNS], local_sem.at[f])
        for f in range(FIELDS)
    ]
    local += [
        pltpu.make_async_copy(flooded_in, flooded.at[0], local_sem.at[4]),
        pltpu.make_async_copy(lateral_in, lateral.at[0], local_sem.at[5]),
        pltpu.make_async_copy(ambient_in, ambient, local_sem.at[6]),
    ]
    for copy in local:
        copy.start()
    for copy in local:
        copy.wait()

    lane = lax.broadcasted_iota(jnp.int32, (ROWS, SPAN), 1)
    sub = lax.broadcasted_iota(jnp.int32, (ROWS, SPAN), 0)
    quad = lane // 4
    place = lane % 4
    tier = sub // COLUMNS
    even = sub % COLUMNS == 0

    def tiled(x):
        return jnp.concatenate([x.astype(jnp.float32)] * LEVELS, axis=0)

    depth_own = tiled(flooded[0])
    mix_own = tiled(lateral[0])
    for f in range(FIELDS):
        def edges(g, acc):
            at = pl.multiple_of(g * ROWS, ROWS)
            return jnp.where(quad == g, pltpu.roll(own[f, pl.ds(at, ROWS)], 4 * g + 2, 1), acc)

        acc = lax.fori_loop(0, groups, edges, jnp.zeros((ROWS, SPAN), jnp.float32), unroll=True)
        if f == 0:
            acc = jnp.where(quad == groups, along(depth_own, 4 * groups + 2), acc)
            acc = jnp.where(quad == groups + 1, along(mix_own, 4 * groups + 6), acc)
        pack[f] = acc

    waits = (
        2 + 3 * inner.astype(jnp.int32) + 3 * above.astype(jnp.int32)
        + top.astype(jnp.int32) + b_other.astype(jnp.int32)
    )
    pl.semaphore_wait(barrier, waits)

    def edge(slot, lon, lat, sent):
        dst = halo_s if slot < 3 else halo_n
        return pltpu.make_async_remote_copy(
            src_ref=pack, dst_ref=dst.at[slot % 3],
            send_sem=edge_send.at[sent], recv_sem=edge_recv.at[slot],
            device_id=(lon, lat), device_id_type=MESH,
        )

    to_a = edge(3, fold_a, row, 6)
    to_b = edge(4, fold_b, row, 7)
    b_copy = pltpu.make_async_copy(pack, halo_n.at[1], local_sem.at[7])
    northward = (edge(0, me, north, 0), edge(1, west, north, 1), edge(2, east, north, 2))
    southward = (edge(3, me, south, 3), edge(4, west, south, 4), edge(5, east, south, 5))

    sides = ((east, west_tile), (west, east_tile))
    statics = [
        [
            pltpu.make_async_remote_copy(
                src_ref=src, dst_ref=dst.at[1 + side],
                send_sem=static_send.at[side, n], recv_sem=static_recv.at[side, n],
                device_id=(lon, row), device_id_type=MESH,
            )
            for n, (src, dst) in enumerate(((flooded_in, flooded), (lateral_in, lateral)))
        ]
        for side, (lon, _) in enumerate(sides)
    ]
    cuts = cuts_of(groups)
    tiles = []
    for c, (first, end) in enumerate(zip(cuts, cuts[1:])):
        lo, hi = first * ROWS, min(end * ROWS, levels * COLUMNS)
        tiles.append([
            [
                pltpu.make_async_remote_copy(
                    src_ref=flat[f].at[lo:hi], dst_ref=dst.at[f, lo:hi],
                    send_sem=ew_send.at[side, c, f], recv_sem=ew_recv.at[side, c, f],
                    device_id=(lon, row), device_id_type=MESH,
                )
                for f in range(FIELDS)
            ]
            for side, (lon, dst) in enumerate(sides)
        ])

    eastward, westward = 0, 1

    def send_tiles(side, chunks):
        for c in chunks:
            for copy in tiles[c][side]:
                copy.start()

    @pl.when(top)
    def _():
        to_a.start()

    @pl.when(b_other)
    def _():
        to_b.start()

    @pl.when(b_self)
    def _():
        b_copy.start()

    @pl.when(inner)
    def _():
        northward[2].start()

    @pl.when(above)
    def _():
        southward[2].start()

    for copy in statics[eastward]:
        copy.start()
    send_tiles(eastward, range(1))

    @pl.when(inner)
    def _():
        northward[0].start()
        northward[1].start()

    @pl.when(above)
    def _():
        southward[0].start()
        southward[1].start()

    send_tiles(eastward, range(1, len(tiles)))
    for copy in statics[westward]:
        copy.start()
    send_tiles(westward, range(len(tiles)))

    for side in statics:
        for copy in side:
            copy.wait_recv()

    @pl.when(above)
    def _():
        for copy in northward:
            copy.wait_recv()

    @pl.when(inner)
    def _():
        for copy in southward:
            copy.wait_recv()

    @pl.when(top)
    def _():
        to_a.wait_recv()

    @pl.when(b_other)
    def _():
        to_b.wait_recv()

    @pl.when(b_self)
    def _():
        b_copy.wait()

    def sideways(o, x):
        return jnp.where(even, up(o, -1), up(x, 1)), jnp.where(even, up(x, -1), up(o, 1))

    def prefix(d):
        two = up(d, COLUMNS)
        s = d + jnp.where(tier >= 1, two, 0.0)
        pair = d + two
        return s + jnp.where(tier >= 2, up(s, 2 * COLUMNS), 0.0), pair + up(pair, 2 * COLUMNS)

    def packed_pressure(t, s):
        inside, total = prefix(0.5 * density(t, s))
        for n in (4, 8, 16, 32, 64):
            total = total + jnp.where(lane >= n, along(total, n), 0.0)
        return inside + jnp.where(lane >= 4, along(total, 4), 0.0)

    def every_quad(x, n):
        x = jnp.where(quad == n, x, 0.0)
        for n in (4, 8, 16, 32, 64):
            x = x + along(x, n)
        return x

    for f in range(FIELDS):
        sign = 1.0 if f < 2 else -1.0
        n0, n1, n2 = halo_n[0, f], halo_n[1, f], halo_n[2, f]
        s0, s1, s2 = halo_s[0, f], halo_s[1, f], halo_s[2, f]
        for dst, n, s, fold in (
            (rim, n0, s0, jnp.where(even, n0, n1)),
            (rim_x, jnp.where(even, n1, n2), jnp.where(even, s1, s2), jnp.where(even, n1, n0)),
        ):
            n = jnp.where(place == 1, along(n, -1), along(n, -3))
            n = jnp.where(top, sign * fold, n)
            s = jnp.where(place == 2, along(s, 1), along(s, 3))
            s = jnp.where(bottom, 0.0, s)
            dst[f] = jnp.where(place < 2, n, s)

    def turning(j):
        total = lat_count * SPAN
        m = jnp.where(j >= total, 2 * total - 1 - j, j)
        return DT * (0.2 + m.astype(jnp.float32) / total)

    def faces(depth, mix, sides_of):
        return [(jnp.minimum(depth, d), mix + m) for d, m in zip(sides_of(0), sides_of(1))]

    def weights(level, depth, around):
        c = [jnp.where(level < d, m, 0.0) for d, m in around]
        return c, 1.0 - ((c[0] + c[1]) + (c[2] + c[3])), level < depth

    def update(weight, turn, cells, e, w, n, s):
        (ce, cw, cn, cs), keep, wet = weight
        half_u = (0.5 * DT) * cells[2]
        half_v = (0.5 * DT) * cells[3]
        ce, cw, cn, cs = ce - half_u, cw + half_u, cn - half_v, cs + half_v
        out = []
        for f in range(FIELDS):
            x = (keep * cells[f] + ce * e[f]) + (cw * w[f] + (cn * n[f] + cs * s[f]))
            if f == 2:
                x = x + (turn * cells[3] - (0.5 * DT) * (e[4] - w[4]))
            if f == 3:
                x = x - (turn * cells[2] + (0.5 * DT) * (n[4] - s[4]))
            out.append(jnp.where(wet, x, 0.0))
        return out

    own_edge = [pack[f] for f in range(FIELDS)]
    cells = [rim[f] for f in range(FIELDS)]
    cells_x = [rim_x[f] for f in range(FIELDS)]
    rim_depth, rim_mix = every_quad(cells[0], groups), (0.5 * DT) * every_quad(cells[0], groups + 1)
    x_depth, x_mix = every_quad(cells_x[0], groups), (0.5 * DT) * every_quad(cells_x[0], groups + 1)
    o_depth, o_mix = every_quad(own_edge[0], groups), (0.5 * DT) * every_quad(own_edge[0], groups + 1)
    for block in (own_edge, cells, cells_x):
        block.append(packed_pressure(block[0], block[1]))
    rim[4] = cells[4]
    rim_x[4] = cells_x[4]

    def around_rim(c, x, o):
        e, w = sideways(c, x)
        return e, w, jnp.where(place == 1, along(c, 1), o), jnp.where(place == 2, along(c, -1), o)

    around = [around_rim(*q) for q in zip(cells, cells_x, own_edge)]
    statics_around = (around_rim(rim_depth, x_depth, o_depth), around_rim(rim_mix, x_mix, o_mix))
    rim_level = (LEVELS * quad + tier).astype(jnp.float32)
    rim_row = jnp.where(place < 2, (row + 1) * SPAN + 1 - place, row * SPAN + 1 - place)
    new = update(
        weights(rim_level, rim_depth, faces(rim_depth, rim_mix, lambda n: statics_around[n])),
        turning(rim_row), cells, *[[q[n] for q in around] for n in range(4)],
    )
    new.append(packed_pressure(new[0], new[1]))
    for q in range(FIELDS + 1):
        rim_new[q] = new[q]

    first_lane = lane == 0
    last_lane = lane == SPAN - 1

    def beside(x, r):
        return jnp.where(last_lane, r, along(x, -1)), jnp.where(first_lane, r, along(x, 1))

    def shifted(x, g):
        return pltpu.roll(x, lax.rem(2 * SPAN - 2 - 4 * g, SPAN) if not isinstance(g, int) else (-2 - 4 * g) % SPAN, 1)

    def around_own(o, x, r):
        return sideways(o, x) + beside(o, r)

    def around_x(o, x, z, r):
        return (jnp.where(even, z, up(o, 1)), jnp.where(even, up(o, -1), z)) + beside(x, r)

    def split(e, w):
        return jnp.where(even, e, w), jnp.where(even, up(e, -1), up(w, 1))

    depth_x, depth_z = split(tiled(flooded[2]), tiled(flooded[1]))
    mix_x, mix_z = split(tiled(lateral[2]), tiled(lateral[1]))
    mix_o, mix_x, mix_z = ((0.5 * DT) * x for x in (mix_own, mix_x, mix_z))
    rim_depth_at, rim_mix_at = shifted(rim_depth, 0), shifted(rim_mix, 0)
    x_depth_at, x_mix_at = shifted(x_depth, 0), shifted(x_mix, 0)
    own_statics = (around_own(depth_own, depth_x, rim_depth_at), around_own(mix_o, mix_x, rim_mix_at))
    x_statics = (
        around_x(depth_own, depth_x, depth_z, x_depth_at), around_x(mix_o, mix_x, mix_z, x_mix_at)
    )
    own_faces = faces(depth_own, mix_o, lambda n: own_statics[n])
    x_faces = faces(depth_x, mix_x, lambda n: x_statics[n])
    turn = turning(row * SPAN + lane)
    ambient_all = tiled(ambient[...])
    tier_level = tier.astype(jnp.float32)
    low = tier % 2 == 0
    lower_half = tier < 2

    def per_level(blocks):
        a, b, c, d = blocks
        ab0, ab1 = jnp.where(low, a, up(b, 2)), jnp.where(low, up(a, -2), b)
        cd0, cd1 = jnp.where(low, c, up(d, 2)), jnp.where(low, up(c, -2), d)
        return (
            jnp.where(lower_half, ab0, up(cd0, 4)), jnp.where(lower_half, ab1, up(cd1, 4)),
            jnp.where(lower_half, up(ab0, 4), cd0), jnp.where(lower_half, up(ab1, 4), cd1),
        )

    def repeated(a):
        ab0, ab1 = jnp.where(low, a, up(a, 2)), jnp.where(low, up(a, -2), a)
        r0, r1 = up(ab0, 4), up(ab1, 4)
        return (
            jnp.where(lower_half, ab0, r0), jnp.where(lower_half, ab1, r1),
            jnp.where(lower_half, r0, ab0), jnp.where(lower_half, r1, ab1),
        )

    def step(g, carry):
        po, px, pz, p2o, p2x, heavy, held, lower, inverse, value = carry
        at = pl.multiple_of(g * ROWS, ROWS)
        o = [own[f, pl.ds(at, ROWS)] for f in range(FIELDS)]
        xz = [split(east_tile[f, pl.ds(at, ROWS)], west_tile[f, pl.ds(at, ROWS)]) for f in range(FIELDS)]
        x, z = [q[0] for q in xz], [q[1] for q in xz]
        pressures = []
        for block, total in ((o, po), (x, px), (z, pz)):
            inside, more = prefix(0.5 * density(block[0], block[1]))
            block.append(inside + total)
            pressures.append(total + more)
        level = tier_level + (LEVELS * g).astype(jnp.float32)
        around = [around_own(*q, shifted(rim[n], g)) for n, q in enumerate(zip(o, x))]
        weight = weights(level, depth_own, own_faces)
        o2 = update(weight, turn, o, *[[q[n] for q in around] for n in range(4)])
        around = [around_x(*q, shifted(rim_x[n], g)) for n, q in enumerate(zip(o, x, z))]
        x2 = update(
            weights(level, depth_x, x_faces), turn, x, *[[q[n] for q in around] for n in range(4)]
        )
        for block, total in ((o2, p2o), (x2, p2x)):
            inside, more = prefix(0.5 * density(block[0], block[1]))
            block.append(inside + total)
            pressures.append(total + more)
        around = [around_own(*q, shifted(rim_new[n], g)) for n, q in enumerate(zip(o2, x2))]
        done = update(weight, turn, o2, *[[q[n] for q in around] for n in range(4)])

        new_heavy = up(density(done[0], done[1]), COLUMNS)
        rise = density(done[0], done[1]) - jnp.where(tier == 0, heavy, new_heavy)
        a = ambient_all * (0.2 + 1.0 / (1.0 + 10.0 * jnp.maximum(rise, 0.0)))
        a = jnp.where(jnp.logical_and(weight[2], level > 0.5), a, 0.0)
        uppers = repeated(a)
        fields = per_level(done)
        xs = (held,) + fields[:3]
        lowers = (lower,) + uppers[:3]
        dets = []
        last, before = None, inverse
        for n in range(LEVELS):
            main = 1.0 + (lowers[n] + uppers[n])
            square = lowers[n] * lowers[n]
            if n == 0:
                det = main - square * before
            elif n == 1:
                det = main * last - square
            else:
                det = main * last - square * before
            dets.append(det)
            last, before = det, last
        ys, rs = [], []
        for n in range(LEVELS):
            inverse = 1.0 / dets[n]
            if n > 0:
                inverse = inverse * dets[n - 1]
            value = (xs[n] + lowers[n] * value) * inverse
            ys.append(value)
            rs.append(uppers[n] * inverse)
        y, r = ys[-1], rs[-1]
        for n in range(LEVELS - 1, -1, -1):
            if n < LEVELS - 1:
                y, r = ys[n] + rs[n] * y, rs[n] * r
            y_out[LEVELS * g + n] = y
            r_out[LEVELS * g + n] = r
        return (*pressures, new_heavy, fields[3], uppers[3], inverse, value)

    zero = jnp.zeros((ROWS, SPAN), jnp.float32)
    carry = (zero,) * 8 + (zero + 1.0, zero)
    for c, (first, end) in enumerate(zip(cuts, cuts[1:])):
        for side in tiles[c]:
            for copy in side:
                copy.wait_recv()
        carry = lax.fori_loop(first, end, step, carry, unroll=2)

    for part in (*tiles, statics):
        for side in part:
            for copy in side:
                copy.wait_send()

    @pl.when(top)
    def _():
        to_a.wait_send()

    @pl.when(b_other)
    def _():
        to_b.wait_send()

    @pl.when(inner)
    def _():
        for copy in northward:
            copy.wait_send()

    @pl.when(above)
    def _():
        for copy in southward:
            copy.wait_send()


def substitute(levels, y, r, t_out, s_out, u_out, v_out, result, sem):
    outs = (t_out, s_out, u_out, v_out)
    groups = pl.cdiv(levels, LEVELS)
    cuts = [0, groups // 3, 2 * groups // 3, groups]
    copies = []
    below = jnp.zeros((ROWS, SPAN), jnp.float32)
    for part in range(len(cuts) - 2, -1, -1):
        for g in range(cuts[part + 1] - 1, cuts[part] - 1, -1):
            at = LEVELS * g
            rows = [y[at + n] + r[at + n] * below for n in range(LEVELS)]
            below = rows[0]
            for n in range(LEVELS):
                if at + n > 0:
                    result[at + n - 1] = rows[n]
        lo = max(LEVELS * cuts[part] - 1, 0)
        hi = LEVELS * cuts[part + 1] - 1
        for f in range(FIELDS):
            copies.append(pltpu.make_async_copy(
                result.at[lo:hi, COLUMNS * f:COLUMNS * (f + 1), :], outs[f].at[lo:hi],
                sem.at[part, f],
            ))
            copies[-1].start()
    for copy in copies:
        copy.wait()


def solution(mesh):
    lon_count, lat_count = mesh.shape["lon"], mesh.shape["lat"]

    def shards(*args):
        levels = args[0].shape[0]
        groups = pl.cdiv(levels, LEVELS)
        chunks = len(cuts_of(groups)) - 1
        f32 = jnp.float32
        vmem = pl.BlockSpec(memory_space=pltpu.VMEM)
        anywhere = pl.BlockSpec(memory_space=pl.ANY)
        y, r = pl.pallas_call(
            functools.partial(halo_and_levels, levels, lon_count, lat_count),
            out_shape=[pltpu.VMEM((groups * LEVELS, ROWS, SPAN), f32)] * 2,
            in_specs=[anywhere] * 7,
            out_specs=[vmem] * 2,
            scratch_shapes=[
                pltpu.VMEM((FIELDS, groups * ROWS, SPAN), f32),
                pltpu.VMEM((FIELDS, groups * ROWS, SPAN), f32),
                pltpu.VMEM((FIELDS, groups * ROWS, SPAN), f32),
                pltpu.VMEM((3, COLUMNS, SPAN), jnp.int32),
                pltpu.VMEM((3, COLUMNS, SPAN), f32),
                pltpu.VMEM((COLUMNS, SPAN), f32),
                pltpu.VMEM((FIELDS, ROWS, SPAN), f32),
                pltpu.VMEM((3, FIELDS, ROWS, SPAN), f32),
                pltpu.VMEM((3, FIELDS, ROWS, SPAN), f32),
                pltpu.VMEM((FIELDS + 1, ROWS, SPAN), f32),
                pltpu.VMEM((FIELDS + 1, ROWS, SPAN), f32),
                pltpu.VMEM((FIELDS + 1, ROWS, SPAN), f32),
                pltpu.SemaphoreType.DMA((8,)),
                pltpu.SemaphoreType.DMA((2, chunks, FIELDS)),
                pltpu.SemaphoreType.DMA((2, chunks, FIELDS)),
                pltpu.SemaphoreType.DMA((2, 2)),
                pltpu.SemaphoreType.DMA((2, 2)),
                pltpu.SemaphoreType.DMA((8,)),
                pltpu.SemaphoreType.DMA((6,)),
            ],
            compiler_params=pltpu.CompilerParams(collective_id=0, has_side_effects=True),
        )(*args)
        return pl.pallas_call(
            functools.partial(substitute, levels),
            out_shape=[jax.ShapeDtypeStruct(args[0].shape, f32)] * FIELDS,
            in_specs=[vmem] * 2,
            out_specs=[anywhere] * FIELDS,
            scratch_shapes=[
                pltpu.VMEM((groups * LEVELS - 1, ROWS, SPAN), f32),
                pltpu.SemaphoreType.DMA((3, FIELDS)),
            ],
        )(*(pltpu.with_memory_space_constraint(q, pltpu.VMEM) for q in (y, r)))

    wide, flat = P(None, "lon", "lat"), P("lon", "lat")
    return jax.shard_map(
        shards,
        mesh=mesh,
        in_specs=(wide,) * 4 + (flat,) * 3,
        out_specs=(wide,) * 4,
        check_vma=False,
    )
```

```python
import functools

import jax
import jax.numpy as jnp
from jax import lax
from jax.experimental import pallas as pl
from jax.experimental.pallas import tpu as pltpu
from jax.sharding import PartitionSpec as P

MESH = pl.DeviceIdType.MESH
DT = 0.05
FIELDS = 4
COLUMNS = 2
SPAN = 128
SEGMENT = 24
LEVELS = 4
ROWS = LEVELS * COLUMNS


def cuts_of(groups):
    return [0, *range(3, groups - 1, 4), groups]


def density(t, s):
    return s * (0.8 + 0.03 * t) - t * (0.2 + 0.05 * t)


def up(x, n):
    return pltpu.roll(x, n % ROWS, 0)


def along(x, n):
    return pltpu.roll(x, n % SPAN, 1)


def halo_and_levels(
    levels, lon_count, lat_count,
    t_in, s_in, u_in, v_in, flooded_in, lateral_in, ambient_in,
    y_out, r_out,
    own, east_tile, west_tile, flooded, lateral, ambient, pack, halo_n, halo_s, rim, rim_x, rim_new,
    local_sem, ew_send, ew_recv, static_send, static_recv, edge_send, edge_recv,
):
    fields_in = (t_in, s_in, u_in, v_in)
    groups = pl.cdiv(levels, LEVELS)
    me = lax.axis_index("lon")
    row = lax.axis_index("lat")
    east = lax.rem(me + 1, lon_count)
    west = lax.rem(me + lon_count - 1, lon_count)
    fold_a = lon_count - 1 - me
    fold_b = lax.rem(2 * lon_count - 2 - me, lon_count)
    top = row == lat_count - 1
    bottom = row == 0
    inner = jnp.logical_not(top)
    above = jnp.logical_not(bottom)
    b_other = jnp.logical_and(top, fold_b != me)
    b_self = jnp.logical_and(top, fold_b == me)
    north = row + 1
    south = row - 1

    barrier = pltpu.get_barrier_semaphore()

    def greet(lon, lat):
        pl.semaphore_signal(barrier, inc=1, device_id=(lon, lat), device_id_type=MESH)

    greet(east, row)
    greet(west, row)

    @pl.when(top)
    def _():
        greet(fold_a, row)

    @pl.when(b_other)
    def _():
        greet(fold_b, row)

    @pl.when(inner)
    def _():
        greet(me, north)
        greet(east, north)
        greet(west, north)

    @pl.when(above)
    def _():
        greet(me, south)
        greet(east, south)
        greet(west, south)

    flat = [x.reshape(levels * COLUMNS, SPAN) for x in fields_in]
    local = [
        pltpu.make_async_copy(flat[f], own.at[f, 0:levels * COLUMNS], local_sem.at[f])
        for f in range(FIELDS)
    ]
    local += [
        pltpu.make_async_copy(flooded_in, flooded.at[0], local_sem.at[4]),
        pltpu.make_async_copy(lateral_in, lateral.at[0], local_sem.at[5]),
        pltpu.make_async_copy(ambient_in, ambient, local_sem.at[6]),
    ]
    for copy in local:
        copy.start()
    for copy in local:
        copy.wait()

    lane = lax.broadcasted_iota(jnp.int32, (ROWS, SPAN), 1)
    sub = lax.broadcasted_iota(jnp.int32, (ROWS, SPAN), 0)
    quad = lane // 4
    place = lane % 4
    tier = sub // COLUMNS
    even = sub % COLUMNS == 0

    def tiled(x):
        return jnp.concatenate([x.astype(jnp.float32)] * LEVELS, axis=0)

    depth_own = tiled(flooded[0])
    mix_own = tiled(lateral[0])
    for f in range(FIELDS):
        def edges(g, acc):
            at = pl.multiple_of(g * ROWS, ROWS)
            return jnp.where(quad == g, pltpu.roll(own[f, pl.ds(at, ROWS)], 4 * g + 2, 1), acc)

        acc = lax.fori_loop(0, groups, edges, jnp.zeros((ROWS, SPAN), jnp.float32), unroll=True)
        if f == 0:
            acc = jnp.where(quad == groups, along(depth_own, 4 * groups + 2), acc)
            acc = jnp.where(quad == groups + 1, along(mix_own, 4 * groups + 6), acc)
        pack[f] = acc

    waits = (
        2 + 3 * inner.astype(jnp.int32) + 3 * above.astype(jnp.int32)
        + top.astype(jnp.int32) + b_other.astype(jnp.int32)
    )
    pl.semaphore_wait(barrier, waits)

    def edge(slot, lon, lat, sent):
        dst = halo_s if slot < 3 else halo_n
        return pltpu.make_async_remote_copy(
            src_ref=pack, dst_ref=dst.at[slot % 3],
            send_sem=edge_send.at[sent], recv_sem=edge_recv.at[slot],
            device_id=(lon, lat), device_id_type=MESH,
        )

    to_a = edge(3, fold_a, row, 6)
    to_b = edge(4, fold_b, row, 7)
    b_copy = pltpu.make_async_copy(pack, halo_n.at[1], local_sem.at[7])
    northward = (edge(0, me, north, 0), edge(1, west, north, 1), edge(2, east, north, 2))
    southward = (edge(3, me, south, 3), edge(4, west, south, 4), edge(5, east, south, 5))

    sides = ((east, west_tile), (west, east_tile))
    statics = [
        [
            pltpu.make_async_remote_copy(
                src_ref=src, dst_ref=dst.at[1 + side],
                send_sem=static_send.at[side, n], recv_sem=static_recv.at[side, n],
                device_id=(lon, row), device_id_type=MESH,
            )
            for n, (src, dst) in enumerate(((flooded_in, flooded), (lateral_in, lateral)))
        ]
        for side, (lon, _) in enumerate(sides)
    ]
    cuts = cuts_of(groups)
    tiles = []
    for c, (first, end) in enumerate(zip(cuts, cuts[1:])):
        lo, hi = first * ROWS, min(end * ROWS, levels * COLUMNS)
        tiles.append([
            pltpu.make_async_remote_copy(
                src_ref=own.at[:, lo:hi], dst_ref=dst.at[:, lo:hi],
                send_sem=ew_send.at[side, c], recv_sem=ew_recv.at[side, c],
                device_id=(lon, row), device_id_type=MESH,
            )
            for side, (lon, dst) in enumerate(sides)
        ])

    eastward, westward = 0, 1

    def send_tiles(side, chunks):
        for c in chunks:
            tiles[c][side].start()

    @pl.when(top)
    def _():
        to_a.start()

    @pl.when(b_other)
    def _():
        to_b.start()

    @pl.when(b_self)
    def _():
        b_copy.start()

    @pl.when(inner)
    def _():
        northward[2].start()

    @pl.when(above)
    def _():
        southward[2].start()

    for copy in statics[eastward]:
        copy.start()
    run_last = lax.rem(me, SEGMENT) == SEGMENT - 1

    @pl.when(run_last)
    def _():
        send_tiles(eastward, range(len(tiles)))

    @pl.when(inner)
    def _():
        northward[0].start()
        northward[1].start()

    @pl.when(above)
    def _():
        southward[0].start()
        southward[1].start()

    @pl.when(jnp.logical_not(run_last))
    def _():
        send_tiles(eastward, range(len(tiles)))

    for copy in statics[westward]:
        copy.start()
    send_tiles(westward, range(len(tiles)))

    for side in statics:
        for copy in side:
            copy.wait_recv()

    @pl.when(above)
    def _():
        for copy in northward:
            copy.wait_recv()

    @pl.when(inner)
    def _():
        for copy in southward:
            copy.wait_recv()

    @pl.when(top)
    def _():
        to_a.wait_recv()

    @pl.when(b_other)
    def _():
        to_b.wait_recv()

    @pl.when(b_self)
    def _():
        b_copy.wait()

    def sideways(o, x):
        return jnp.where(even, up(o, -1), up(x, 1)), jnp.where(even, up(x, -1), up(o, 1))

    def prefix(d):
        two = up(d, COLUMNS)
        s = d + jnp.where(tier >= 1, two, 0.0)
        pair = d + two
        return s + jnp.where(tier >= 2, up(s, 2 * COLUMNS), 0.0), pair + up(pair, 2 * COLUMNS)

    def packed_pressure(t, s):
        inside, total = prefix(0.5 * density(t, s))
        for n in (4, 8, 16, 32, 64):
            total = total + jnp.where(lane >= n, along(total, n), 0.0)
        return inside + jnp.where(lane >= 4, along(total, 4), 0.0)

    def every_quad(x, n):
        x = jnp.where(quad == n, x, 0.0)
        for n in (4, 8, 16, 32, 64):
            x = x + along(x, n)
        return x

    for f in range(FIELDS):
        sign = 1.0 if f < 2 else -1.0
        n0, n1, n2 = halo_n[0, f], halo_n[1, f], halo_n[2, f]
        s0, s1, s2 = halo_s[0, f], halo_s[1, f], halo_s[2, f]
        for dst, n, s, fold in (
            (rim, n0, s0, jnp.where(even, n0, n1)),
            (rim_x, jnp.where(even, n1, n2), jnp.where(even, s1, s2), jnp.where(even, n1, n0)),
        ):
            n = jnp.where(place == 1, along(n, -1), along(n, -3))
            n = jnp.where(top, sign * fold, n)
            s = jnp.where(place == 2, along(s, 1), along(s, 3))
            s = jnp.where(bottom, 0.0, s)
            dst[f] = jnp.where(place < 2, n, s)

    def turning(j):
        total = lat_count * SPAN
        m = jnp.where(j >= total, 2 * total - 1 - j, j)
        return DT * (0.2 + m.astype(jnp.float32) / total)

    def faces(depth, mix, sides_of):
        return [(jnp.minimum(depth, d), mix + m) for d, m in zip(sides_of(0), sides_of(1))]

    def weights(level, depth, around):
        c = [jnp.where(level < d, m, 0.0) for d, m in around]
        return c, 1.0 - ((c[0] + c[1]) + (c[2] + c[3])), level < depth

    def update(weight, turn, cells, e, w, n, s):
        (ce, cw, cn, cs), keep, wet = weight
        half_u = (0.5 * DT) * cells[2]
        half_v = (0.5 * DT) * cells[3]
        ce, cw, cn, cs = ce - half_u, cw + half_u, cn - half_v, cs + half_v
        out = []
        for f in range(FIELDS):
            x = (keep * cells[f] + ce * e[f]) + (cw * w[f] + (cn * n[f] + cs * s[f]))
            if f == 2:
                x = x + (turn * cells[3] - (0.5 * DT) * (e[4] - w[4]))
            if f == 3:
                x = x - (turn * cells[2] + (0.5 * DT) * (n[4] - s[4]))
            out.append(jnp.where(wet, x, 0.0))
        return out

    own_edge = [pack[f] for f in range(FIELDS)]
    cells = [rim[f] for f in range(FIELDS)]
    cells_x = [rim_x[f] for f in range(FIELDS)]
    rim_depth, rim_mix = every_quad(cells[0], groups), (0.5 * DT) * every_quad(cells[0], groups + 1)
    x_depth, x_mix = every_quad(cells_x[0], groups), (0.5 * DT) * every_quad(cells_x[0], groups + 1)
    o_depth, o_mix = every_quad(own_edge[0], groups), (0.5 * DT) * every_quad(own_edge[0], groups + 1)
    for block in (own_edge, cells, cells_x):
        block.append(packed_pressure(block[0], block[1]))
    rim[4] = cells[4]
    rim_x[4] = cells_x[4]

    def around_rim(c, x, o):
        e, w = sideways(c, x)
        return e, w, jnp.where(place == 1, along(c, 1), o), jnp.where(place == 2, along(c, -1), o)

    around = [around_rim(*q) for q in zip(cells, cells_x, own_edge)]
    statics_around = (around_rim(rim_depth, x_depth, o_depth), around_rim(rim_mix, x_mix, o_mix))
    rim_level = (LEVELS * quad + tier).astype(jnp.float32)
    rim_row = jnp.where(place < 2, (row + 1) * SPAN + 1 - place, row * SPAN + 1 - place)
    new = update(
        weights(rim_level, rim_depth, faces(rim_depth, rim_mix, lambda n: statics_around[n])),
        turning(rim_row), cells, *[[q[n] for q in around] for n in range(4)],
    )
    new.append(packed_pressure(new[0], new[1]))
    for q in range(FIELDS + 1):
        rim_new[q] = new[q]

    first_lane = lane == 0
    last_lane = lane == SPAN - 1

    def beside(x, r):
        return jnp.where(last_lane, r, along(x, -1)), jnp.where(first_lane, r, along(x, 1))

    def shifted(x, g):
        return pltpu.roll(x, lax.rem(2 * SPAN - 2 - 4 * g, SPAN) if not isinstance(g, int) else (-2 - 4 * g) % SPAN, 1)

    def around_own(o, x, r):
        return sideways(o, x) + beside(o, r)

    def around_x(o, x, z, r):
        return (jnp.where(even, z, up(o, 1)), jnp.where(even, up(o, -1), z)) + beside(x, r)

    def split(e, w):
        return jnp.where(even, e, w), jnp.where(even, up(e, -1), up(w, 1))

    depth_x, depth_z = split(tiled(flooded[2]), tiled(flooded[1]))
    mix_x, mix_z = split(tiled(lateral[2]), tiled(lateral[1]))
    mix_o, mix_x, mix_z = ((0.5 * DT) * x for x in (mix_own, mix_x, mix_z))
    rim_depth_at, rim_mix_at = shifted(rim_depth, 0), shifted(rim_mix, 0)
    x_depth_at, x_mix_at = shifted(x_depth, 0), shifted(x_mix, 0)
    own_statics = (around_own(depth_own, depth_x, rim_depth_at), around_own(mix_o, mix_x, rim_mix_at))
    x_statics = (
        around_x(depth_own, depth_x, depth_z, x_depth_at), around_x(mix_o, mix_x, mix_z, x_mix_at)
    )
    own_faces = faces(depth_own, mix_o, lambda n: own_statics[n])
    x_faces = faces(depth_x, mix_x, lambda n: x_statics[n])
    turn = turning(row * SPAN + lane)
    ambient_all = tiled(ambient[...])
    tier_level = tier.astype(jnp.float32)
    low = tier % 2 == 0
    lower_half = tier < 2

    def per_level(blocks):
        a, b, c, d = blocks
        ab0, ab1 = jnp.where(low, a, up(b, 2)), jnp.where(low, up(a, -2), b)
        cd0, cd1 = jnp.where(low, c, up(d, 2)), jnp.where(low, up(c, -2), d)
        return (
            jnp.where(lower_half, ab0, up(cd0, 4)), jnp.where(lower_half, ab1, up(cd1, 4)),
            jnp.where(lower_half, up(ab0, 4), cd0), jnp.where(lower_half, up(ab1, 4), cd1),
        )

    def repeated(a):
        ab0, ab1 = jnp.where(low, a, up(a, 2)), jnp.where(low, up(a, -2), a)
        r0, r1 = up(ab0, 4), up(ab1, 4)
        return (
            jnp.where(lower_half, ab0, r0), jnp.where(lower_half, ab1, r1),
            jnp.where(lower_half, r0, ab0), jnp.where(lower_half, r1, ab1),
        )

    def step(g, carry):
        po, px, pz, p2o, p2x, heavy, held, lower, inverse, value = carry
        at = pl.multiple_of(g * ROWS, ROWS)
        o = [own[f, pl.ds(at, ROWS)] for f in range(FIELDS)]
        xz = [split(east_tile[f, pl.ds(at, ROWS)], west_tile[f, pl.ds(at, ROWS)]) for f in range(FIELDS)]
        x, z = [q[0] for q in xz], [q[1] for q in xz]
        pressures = []
        for block, total in ((o, po), (x, px), (z, pz)):
            inside, more = prefix(0.5 * density(block[0], block[1]))
            block.append(inside + total)
            pressures.append(total + more)
        level = tier_level + (LEVELS * g).astype(jnp.float32)
        around = [around_own(*q, shifted(rim[n], g)) for n, q in enumerate(zip(o, x))]
        weight = weights(level, depth_own, own_faces)
        o2 = update(weight, turn, o, *[[q[n] for q in around] for n in range(4)])
        around = [around_x(*q, shifted(rim_x[n], g)) for n, q in enumerate(zip(o, x, z))]
        x2 = update(
            weights(level, depth_x, x_faces), turn, x, *[[q[n] for q in around] for n in range(4)]
        )
        for block, total in ((o2, p2o), (x2, p2x)):
            inside, more = prefix(0.5 * density(block[0], block[1]))
            block.append(inside + total)
            pressures.append(total + more)
        around = [around_own(*q, shifted(rim_new[n], g)) for n, q in enumerate(zip(o2, x2))]
        done = update(weight, turn, o2, *[[q[n] for q in around] for n in range(4)])

        new_heavy = up(density(done[0], done[1]), COLUMNS)
        rise = density(done[0], done[1]) - jnp.where(tier == 0, heavy, new_heavy)
        a = ambient_all * (0.2 + 1.0 / (1.0 + 10.0 * jnp.maximum(rise, 0.0)))
        a = jnp.where(jnp.logical_and(weight[2], level > 0.5), a, 0.0)
        uppers = repeated(a)
        fields = per_level(done)
        xs = (held,) + fields[:3]
        lowers = (lower,) + uppers[:3]
        dets = []
        last, before = None, inverse
        for n in range(LEVELS):
            main = 1.0 + (lowers[n] + uppers[n])
            square = lowers[n] * lowers[n]
            if n == 0:
                det = main - square * before
            elif n == 1:
                det = main * last - square
            else:
                det = main * last - square * before
            dets.append(det)
            last, before = det, last
        ys, rs = [], []
        for n in range(LEVELS):
            inverse = 1.0 / dets[n]
            if n > 0:
                inverse = inverse * dets[n - 1]
            value = (xs[n] + lowers[n] * value) * inverse
            ys.append(value)
            rs.append(uppers[n] * inverse)
        y, r = ys[-1], rs[-1]
        for n in range(LEVELS - 1, -1, -1):
            if n < LEVELS - 1:
                y, r = ys[n] + rs[n] * y, rs[n] * r
            y_out[LEVELS * g + n] = y
            r_out[LEVELS * g + n] = r
        return (*pressures, new_heavy, fields[3], uppers[3], inverse, value)

    zero = jnp.zeros((ROWS, SPAN), jnp.float32)
    carry = (zero,) * 8 + (zero + 1.0, zero)
    for c, (first, end) in enumerate(zip(cuts, cuts[1:])):
        for copy in tiles[c]:
            copy.wait_recv()
        carry = lax.fori_loop(first, end, step, carry, unroll=2)

    for part in (*tiles, *statics):
        for copy in part:
            copy.wait_send()

    @pl.when(top)
    def _():
        to_a.wait_send()

    @pl.when(b_other)
    def _():
        to_b.wait_send()

    @pl.when(inner)
    def _():
        for copy in northward:
            copy.wait_send()

    @pl.when(above)
    def _():
        for copy in southward:
            copy.wait_send()


def substitute(levels, y, r, t_out, s_out, u_out, v_out, result, sem):
    outs = (t_out, s_out, u_out, v_out)
    groups = pl.cdiv(levels, LEVELS)
    cuts = [0, groups // 3, 2 * groups // 3, groups]
    copies = []
    below = jnp.zeros((ROWS, SPAN), jnp.float32)
    for part in range(len(cuts) - 2, -1, -1):
        for g in range(cuts[part + 1] - 1, cuts[part] - 1, -1):
            at = LEVELS * g
            rows = [y[at + n] + r[at + n] * below for n in range(LEVELS)]
            below = rows[0]
            for n in range(LEVELS):
                if at + n > 0:
                    result[at + n - 1] = rows[n]
        lo = max(LEVELS * cuts[part] - 1, 0)
        hi = LEVELS * cuts[part + 1] - 1
        for f in range(FIELDS):
            copies.append(pltpu.make_async_copy(
                result.at[lo:hi, COLUMNS * f:COLUMNS * (f + 1), :], outs[f].at[lo:hi],
                sem.at[part, f],
            ))
            copies[-1].start()
    for copy in copies:
        copy.wait()


def solution(mesh):
    lon_count, lat_count = mesh.shape["lon"], mesh.shape["lat"]

    def shards(*args):
        levels = args[0].shape[0]
        groups = pl.cdiv(levels, LEVELS)
        chunks = len(cuts_of(groups)) - 1
        f32 = jnp.float32
        vmem = pl.BlockSpec(memory_space=pltpu.VMEM)
        anywhere = pl.BlockSpec(memory_space=pl.ANY)
        y, r = pl.pallas_call(
            functools.partial(halo_and_levels, levels, lon_count, lat_count),
            out_shape=[pltpu.VMEM((groups * LEVELS, ROWS, SPAN), f32)] * 2,
            in_specs=[anywhere] * 7,
            out_specs=[vmem] * 2,
            scratch_shapes=[
                pltpu.VMEM((FIELDS, groups * ROWS, SPAN), f32),
                pltpu.VMEM((FIELDS, groups * ROWS, SPAN), f32),
                pltpu.VMEM((FIELDS, groups * ROWS, SPAN), f32),
                pltpu.VMEM((3, COLUMNS, SPAN), jnp.int32),
                pltpu.VMEM((3, COLUMNS, SPAN), f32),
                pltpu.VMEM((COLUMNS, SPAN), f32),
                pltpu.VMEM((FIELDS, ROWS, SPAN), f32),
                pltpu.VMEM((3, FIELDS, ROWS, SPAN), f32),
                pltpu.VMEM((3, FIELDS, ROWS, SPAN), f32),
                pltpu.VMEM((FIELDS + 1, ROWS, SPAN), f32),
                pltpu.VMEM((FIELDS + 1, ROWS, SPAN), f32),
                pltpu.VMEM((FIELDS + 1, ROWS, SPAN), f32),
                pltpu.SemaphoreType.DMA((8,)),
                pltpu.SemaphoreType.DMA((2, chunks)),
                pltpu.SemaphoreType.DMA((2, chunks)),
                pltpu.SemaphoreType.DMA((2, 2)),
                pltpu.SemaphoreType.DMA((2, 2)),
                pltpu.SemaphoreType.DMA((8,)),
                pltpu.SemaphoreType.DMA((6,)),
            ],
            compiler_params=pltpu.CompilerParams(collective_id=0, has_side_effects=True),
        )(*args)
        return pl.pallas_call(
            functools.partial(substitute, levels),
            out_shape=[jax.ShapeDtypeStruct(args[0].shape, f32)] * FIELDS,
            in_specs=[vmem] * 2,
            out_specs=[anywhere] * FIELDS,
            scratch_shapes=[
                pltpu.VMEM((groups * LEVELS - 1, ROWS, SPAN), f32),
                pltpu.SemaphoreType.DMA((3, FIELDS)),
            ],
        )(*(pltpu.with_memory_space_constraint(q, pltpu.VMEM) for q in (y, r)))

    wide, flat = P(None, "lon", "lat"), P("lon", "lat")
    return jax.shard_map(
        shards,
        mesh=mesh,
        in_specs=(wide,) * 4 + (flat,) * 3,
        out_specs=(wide,) * 4,
        check_vma=False,
    )
```

```python
import functools

import jax
import jax.numpy as jnp
from jax import lax
from jax.experimental import pallas as pl
from jax.experimental.pallas import tpu as pltpu
from jax.sharding import PartitionSpec as P

MESH = pl.DeviceIdType.MESH
DT = 0.05
FIELDS = 4
COLUMNS = 2
SPAN = 128
SEGMENT = 24
LEVELS = 4
ROWS = LEVELS * COLUMNS


def cuts_of(groups):
    return [0, *range(3, groups - 1, 4), groups]


def density(t, s):
    return s * (0.8 + 0.03 * t) - t * (0.2 + 0.05 * t)


def up(x, n):
    return pltpu.roll(x, n % ROWS, 0)


def along(x, n):
    return pltpu.roll(x, n % SPAN, 1)


def halo_and_levels(
    levels, lon_count, lat_count,
    t_in, s_in, u_in, v_in, flooded_in, lateral_in, ambient_in,
    y_out, r_out,
    own, east_tile, west_tile, flooded, lateral, ambient, pack, halo_n, halo_s, rim, rim_x, rim_new,
    local_sem, ew_send, ew_recv, static_send, static_recv, edge_send, edge_recv,
):
    fields_in = (t_in, s_in, u_in, v_in)
    groups = pl.cdiv(levels, LEVELS)
    me = lax.axis_index("lon")
    row = lax.axis_index("lat")
    east = lax.rem(me + 1, lon_count)
    west = lax.rem(me + lon_count - 1, lon_count)
    fold_a = lon_count - 1 - me
    fold_b = lax.rem(2 * lon_count - 2 - me, lon_count)
    top = row == lat_count - 1
    bottom = row == 0
    inner = jnp.logical_not(top)
    above = jnp.logical_not(bottom)
    b_other = jnp.logical_and(top, fold_b != me)
    b_self = jnp.logical_and(top, fold_b == me)
    north = row + 1
    south = row - 1

    barrier = pltpu.get_barrier_semaphore()

    def greet(lon, lat):
        pl.semaphore_signal(barrier, inc=1, device_id=(lon, lat), device_id_type=MESH)

    @pl.when(inner)
    def _():
        greet(me, north)
        greet(west, north)
        greet(east, north)

    @pl.when(above)
    def _():
        greet(me, south)
        greet(west, south)
        greet(east, south)

    greet(west, row)
    greet(east, row)

    @pl.when(top)
    def _():
        greet(fold_a, row)

    @pl.when(b_other)
    def _():
        greet(fold_b, row)

    flat = [x.reshape(levels * COLUMNS, SPAN) for x in fields_in]
    local = [
        pltpu.make_async_copy(flat[f], own.at[f, 0:levels * COLUMNS], local_sem.at[f])
        for f in range(FIELDS)
    ]
    local += [
        pltpu.make_async_copy(flooded_in, flooded.at[0], local_sem.at[4]),
        pltpu.make_async_copy(lateral_in, lateral.at[0], local_sem.at[5]),
        pltpu.make_async_copy(ambient_in, ambient, local_sem.at[6]),
    ]
    for copy in local:
        copy.start()
    for copy in local:
        copy.wait()

    lane = lax.broadcasted_iota(jnp.int32, (ROWS, SPAN), 1)
    sub = lax.broadcasted_iota(jnp.int32, (ROWS, SPAN), 0)
    quad = lane // 4
    place = lane % 4
    tier = sub // COLUMNS
    even = sub % COLUMNS == 0

    def tiled(x):
        return jnp.concatenate([x.astype(jnp.float32)] * LEVELS, axis=0)

    depth_own = tiled(flooded[0])
    mix_own = tiled(lateral[0])
    for f in range(FIELDS):
        def edges(g, acc):
            at = pl.multiple_of(g * ROWS, ROWS)
            return jnp.where(quad == g, pltpu.roll(own[f, pl.ds(at, ROWS)], 4 * g + 2, 1), acc)

        acc = lax.fori_loop(0, groups, edges, jnp.zeros((ROWS, SPAN), jnp.float32), unroll=True)
        if f == 0:
            acc = jnp.where(quad == groups, along(depth_own, 4 * groups + 2), acc)
            acc = jnp.where(quad == groups + 1, along(mix_own, 4 * groups + 6), acc)
        pack[f] = acc

    waits = (
        2 + 3 * inner.astype(jnp.int32) + 3 * above.astype(jnp.int32)
        + top.astype(jnp.int32) + b_other.astype(jnp.int32)
    )
    pl.semaphore_wait(barrier, waits)

    def edge(slot, lon, lat, sent):
        dst = halo_s if slot < 3 else halo_n
        return pltpu.make_async_remote_copy(
            src_ref=pack, dst_ref=dst.at[slot % 3],
            send_sem=edge_send.at[sent], recv_sem=edge_recv.at[slot],
            device_id=(lon, lat), device_id_type=MESH,
        )

    to_a = edge(3, fold_a, row, 6)
    to_b = edge(4, fold_b, row, 7)
    b_copy = pltpu.make_async_copy(pack, halo_n.at[1], local_sem.at[7])
    northward = (edge(0, me, north, 0), edge(1, west, north, 1), edge(2, east, north, 2))
    southward = (edge(3, me, south, 3), edge(4, west, south, 4), edge(5, east, south, 5))

    sides = ((east, west_tile), (west, east_tile))
    statics = [
        [
            pltpu.make_async_remote_copy(
                src_ref=src, dst_ref=dst.at[1 + side],
                send_sem=static_send.at[side, n], recv_sem=static_recv.at[side, n],
                device_id=(lon, row), device_id_type=MESH,
            )
            for n, (src, dst) in enumerate(((flooded_in, flooded), (lateral_in, lateral)))
        ]
        for side, (lon, _) in enumerate(sides)
    ]
    cuts = cuts_of(groups)
    tiles = []
    for c, (first, end) in enumerate(zip(cuts, cuts[1:])):
        lo, hi = first * ROWS, min(end * ROWS, levels * COLUMNS)
        tiles.append([
            pltpu.make_async_remote_copy(
                src_ref=own.at[:, lo:hi], dst_ref=dst.at[:, lo:hi],
                send_sem=ew_send.at[side, c], recv_sem=ew_recv.at[side, c],
                device_id=(lon, row), device_id_type=MESH,
            )
            for side, (lon, dst) in enumerate(sides)
        ])

    eastward, westward = 0, 1

    def send_tiles(side, chunks):
        for c in chunks:
            tiles[c][side].start()

    @pl.when(top)
    def _():
        to_a.start()

    @pl.when(b_other)
    def _():
        to_b.start()

    @pl.when(b_self)
    def _():
        b_copy.start()

    @pl.when(inner)
    def _():
        northward[2].start()

    @pl.when(above)
    def _():
        southward[2].start()

    for copy in statics[eastward]:
        copy.start()
    run_last = lax.rem(me, SEGMENT) == SEGMENT - 1

    @pl.when(run_last)
    def _():
        send_tiles(eastward, range(len(tiles)))

    @pl.when(inner)
    def _():
        northward[0].start()
        northward[1].start()

    @pl.when(above)
    def _():
        southward[0].start()
        southward[1].start()

    @pl.when(jnp.logical_not(run_last))
    def _():
        send_tiles(eastward, range(len(tiles)))

    for copy in statics[westward]:
        copy.start()
    send_tiles(westward, range(len(tiles)))

    for side in statics:
        for copy in side:
            copy.wait_recv()

    @pl.when(above)
    def _():
        for copy in northward:
            copy.wait_recv()

    @pl.when(inner)
    def _():
        for copy in southward:
            copy.wait_recv()

    @pl.when(top)
    def _():
        to_a.wait_recv()

    @pl.when(b_other)
    def _():
        to_b.wait_recv()

    @pl.when(b_self)
    def _():
        b_copy.wait()

    def sideways(o, x):
        return jnp.where(even, up(o, -1), up(x, 1)), jnp.where(even, up(x, -1), up(o, 1))

    def prefix(d):
        two = up(d, COLUMNS)
        s = d + jnp.where(tier >= 1, two, 0.0)
        pair = d + two
        return s + jnp.where(tier >= 2, up(s, 2 * COLUMNS), 0.0), pair + up(pair, 2 * COLUMNS)

    def packed_pressure(t, s):
        inside, total = prefix((0.25 * DT) * density(t, s))
        for n in (4, 8, 16, 32, 64):
            total = total + jnp.where(lane >= n, along(total, n), 0.0)
        return inside + jnp.where(lane >= 4, along(total, 4), 0.0)

    def every_quad(x, n):
        x = jnp.where(quad == n, x, 0.0)
        for n in (4, 8, 16, 32, 64):
            x = x + along(x, n)
        return x

    for f in range(FIELDS):
        sign = 1.0 if f < 2 else -1.0
        n0, n1, n2 = halo_n[0, f], halo_n[1, f], halo_n[2, f]
        s0, s1, s2 = halo_s[0, f], halo_s[1, f], halo_s[2, f]
        for dst, n, s, fold in (
            (rim, n0, s0, jnp.where(even, n0, n1)),
            (rim_x, jnp.where(even, n1, n2), jnp.where(even, s1, s2), jnp.where(even, n1, n0)),
        ):
            n = jnp.where(place == 1, along(n, -1), along(n, -3))
            n = jnp.where(top, sign * fold, n)
            s = jnp.where(place == 2, along(s, 1), along(s, 3))
            s = jnp.where(bottom, 0.0, s)
            dst[f] = jnp.where(place < 2, n, s)

    def turning(j):
        total = lat_count * SPAN
        m = jnp.where(j >= total, 2 * total - 1 - j, j)
        return DT * (0.2 + m.astype(jnp.float32) / total)

    def faces(depth, mix, sides_of):
        return [(jnp.minimum(depth, d), mix + m) for d, m in zip(sides_of(0), sides_of(1))]

    def weights(level, depth, around):
        c = [jnp.where(level < d, m, 0.0) for d, m in around]
        return c, 1.0 - ((c[0] + c[1]) + (c[2] + c[3])), level < depth

    def update(weight, turn, cells, e, w, n, s):
        (ce, cw, cn, cs), keep, wet = weight
        half_u = (0.5 * DT) * cells[2]
        half_v = (0.5 * DT) * cells[3]
        ce, cw, cn, cs = ce - half_u, cw + half_u, cn - half_v, cs + half_v
        out = []
        for f in range(FIELDS):
            x = (keep * cells[f] + ce * e[f]) + (cw * w[f] + (cn * n[f] + cs * s[f]))
            if f == 2:
                x = x + (turn * cells[3] - (e[4] - w[4]))
            if f == 3:
                x = x - (turn * cells[2] + (n[4] - s[4]))
            out.append(jnp.where(wet, x, 0.0))
        return out

    own_edge = [pack[f] for f in range(FIELDS)]
    cells = [rim[f] for f in range(FIELDS)]
    cells_x = [rim_x[f] for f in range(FIELDS)]
    rim_depth, rim_mix = every_quad(cells[0], groups), (0.5 * DT) * every_quad(cells[0], groups + 1)
    x_depth, x_mix = every_quad(cells_x[0], groups), (0.5 * DT) * every_quad(cells_x[0], groups + 1)
    o_depth, o_mix = every_quad(own_edge[0], groups), (0.5 * DT) * every_quad(own_edge[0], groups + 1)
    for block in (own_edge, cells, cells_x):
        block.append(packed_pressure(block[0], block[1]))
    rim[4] = cells[4]
    rim_x[4] = cells_x[4]

    def around_rim(c, x, o):
        e, w = sideways(c, x)
        return e, w, jnp.where(place == 1, along(c, 1), o), jnp.where(place == 2, along(c, -1), o)

    around = [around_rim(*q) for q in zip(cells, cells_x, own_edge)]
    statics_around = (around_rim(rim_depth, x_depth, o_depth), around_rim(rim_mix, x_mix, o_mix))
    rim_level = (LEVELS * quad + tier).astype(jnp.float32)
    rim_row = jnp.where(place < 2, (row + 1) * SPAN + 1 - place, row * SPAN + 1 - place)
    new = update(
        weights(rim_level, rim_depth, faces(rim_depth, rim_mix, lambda n: statics_around[n])),
        turning(rim_row), cells, *[[q[n] for q in around] for n in range(4)],
    )
    new.append(packed_pressure(new[0], new[1]))
    for q in range(FIELDS + 1):
        rim_new[q] = new[q]

    first_lane = lane == 0
    last_lane = lane == SPAN - 1

    def beside(x, r):
        return jnp.where(last_lane, r, along(x, -1)), jnp.where(first_lane, r, along(x, 1))

    def shifted(x, g):
        return pltpu.roll(x, lax.rem(2 * SPAN - 2 - 4 * g, SPAN) if not isinstance(g, int) else (-2 - 4 * g) % SPAN, 1)

    def around_own(o, x, r):
        return sideways(o, x) + beside(o, r)

    def around_x(o, x, z, r):
        return (jnp.where(even, z, up(o, 1)), jnp.where(even, up(o, -1), z)) + beside(x, r)

    def split(e, w):
        return jnp.where(even, e, w), jnp.where(even, up(e, -1), up(w, 1))

    depth_x, depth_z = split(tiled(flooded[2]), tiled(flooded[1]))
    mix_x, mix_z = split(tiled(lateral[2]), tiled(lateral[1]))
    mix_o, mix_x, mix_z = ((0.5 * DT) * x for x in (mix_own, mix_x, mix_z))
    rim_depth_at, rim_mix_at = shifted(rim_depth, 0), shifted(rim_mix, 0)
    x_depth_at, x_mix_at = shifted(x_depth, 0), shifted(x_mix, 0)
    own_statics = (around_own(depth_own, depth_x, rim_depth_at), around_own(mix_o, mix_x, rim_mix_at))
    x_statics = (
        around_x(depth_own, depth_x, depth_z, x_depth_at), around_x(mix_o, mix_x, mix_z, x_mix_at)
    )
    own_faces = faces(depth_own, mix_o, lambda n: own_statics[n])
    x_faces = faces(depth_x, mix_x, lambda n: x_statics[n])
    turn = turning(row * SPAN + lane)
    ambient_all = tiled(ambient[...])
    tier_level = tier.astype(jnp.float32)
    low = tier % 2 == 0
    lower_half = tier < 2

    def per_level(blocks):
        a, b, c, d = blocks
        ab0, ab1 = jnp.where(low, a, up(b, 2)), jnp.where(low, up(a, -2), b)
        cd0, cd1 = jnp.where(low, c, up(d, 2)), jnp.where(low, up(c, -2), d)
        return (
            jnp.where(lower_half, ab0, up(cd0, 4)), jnp.where(lower_half, ab1, up(cd1, 4)),
            jnp.where(lower_half, up(ab0, 4), cd0), jnp.where(lower_half, up(ab1, 4), cd1),
        )

    def repeated(a):
        ab0, ab1 = jnp.where(low, a, up(a, 2)), jnp.where(low, up(a, -2), a)
        r0, r1 = up(ab0, 4), up(ab1, 4)
        return (
            jnp.where(lower_half, ab0, r0), jnp.where(lower_half, ab1, r1),
            jnp.where(lower_half, r0, ab0), jnp.where(lower_half, r1, ab1),
        )

    def step(g, carry):
        po, px, pz, p2o, p2x, heavy, held, lower, inverse, value = carry
        at = pl.multiple_of(g * ROWS, ROWS)
        o = [own[f, pl.ds(at, ROWS)] for f in range(FIELDS)]
        xz = [split(east_tile[f, pl.ds(at, ROWS)], west_tile[f, pl.ds(at, ROWS)]) for f in range(FIELDS)]
        x, z = [q[0] for q in xz], [q[1] for q in xz]
        pressures = []
        for block, total in ((o, po), (x, px), (z, pz)):
            inside, more = prefix((0.25 * DT) * density(block[0], block[1]))
            block.append(inside + total)
            pressures.append(total + more)
        level = tier_level + (LEVELS * g).astype(jnp.float32)
        around = [around_own(*q, shifted(rim[n], g)) for n, q in enumerate(zip(o, x))]
        weight = weights(level, depth_own, own_faces)
        o2 = update(weight, turn, o, *[[q[n] for q in around] for n in range(4)])
        around = [around_x(*q, shifted(rim_x[n], g)) for n, q in enumerate(zip(o, x, z))]
        x2 = update(
            weights(level, depth_x, x_faces), turn, x, *[[q[n] for q in around] for n in range(4)]
        )
        for block, total in ((o2, p2o), (x2, p2x)):
            inside, more = prefix((0.25 * DT) * density(block[0], block[1]))
            block.append(inside + total)
            pressures.append(total + more)
        around = [around_own(*q, shifted(rim_new[n], g)) for n, q in enumerate(zip(o2, x2))]
        done = update(weight, turn, o2, *[[q[n] for q in around] for n in range(4)])

        weighed = density(done[0], done[1])
        new_heavy = up(weighed, COLUMNS)
        rise = weighed - jnp.where(tier == 0, heavy, new_heavy)
        a = ambient_all * (0.2 + 1.0 / (1.0 + 10.0 * jnp.maximum(rise, 0.0)))
        a = jnp.where(jnp.logical_and(weight[2], level > 0.5), a, 0.0)
        uppers = repeated(a)
        fields = per_level(done)
        xs = (held,) + fields[:3]
        lowers = (lower,) + uppers[:3]
        dets = []
        last, before = None, inverse
        for n in range(LEVELS):
            main = 1.0 + (lowers[n] + uppers[n])
            square = lowers[n] * lowers[n]
            if n == 0:
                det = main - square * before
            elif n == 1:
                det = main * last - square
            else:
                det = main * last - square * before
            dets.append(det)
            last, before = det, last
        ys, rs = [], []
        for n in range(LEVELS):
            inverse = 1.0 / dets[n]
            if n > 0:
                inverse = inverse * dets[n - 1]
            value = (xs[n] + lowers[n] * value) * inverse
            ys.append(value)
            rs.append(uppers[n] * inverse)
        y, r = ys[-1], rs[-1]
        for n in range(LEVELS - 1, -1, -1):
            if n < LEVELS - 1:
                y, r = ys[n] + rs[n] * y, rs[n] * r
            y_out[LEVELS * g + n] = y
            r_out[LEVELS * g + n] = r
        return (*pressures, new_heavy, fields[3], uppers[3], inverse, value)

    zero = jnp.zeros((ROWS, SPAN), jnp.float32)
    carry = (zero,) * 8 + (zero + 1.0, zero)
    for c, (first, end) in enumerate(zip(cuts, cuts[1:])):
        for copy in tiles[c]:
            copy.wait_recv()
        carry = lax.fori_loop(first, end, step, carry, unroll=2)

    for part in (*tiles, *statics):
        for copy in part:
            copy.wait_send()

    @pl.when(top)
    def _():
        to_a.wait_send()

    @pl.when(b_other)
    def _():
        to_b.wait_send()

    @pl.when(inner)
    def _():
        for copy in northward:
            copy.wait_send()

    @pl.when(above)
    def _():
        for copy in southward:
            copy.wait_send()


def substitute(levels, y, r, t_out, s_out, u_out, v_out, result, sem):
    outs = (t_out, s_out, u_out, v_out)
    groups = pl.cdiv(levels, LEVELS)
    cuts = [0, groups // 3, 2 * groups // 3, groups]
    copies = []
    below = jnp.zeros((ROWS, SPAN), jnp.float32)
    for part in range(len(cuts) - 2, -1, -1):
        for g in range(cuts[part + 1] - 1, cuts[part] - 1, -1):
            at = LEVELS * g
            rows = [y[at + n] + r[at + n] * below for n in range(LEVELS)]
            below = rows[0]
            for n in range(LEVELS):
                if at + n > 0:
                    result[at + n - 1] = rows[n]
        lo = max(LEVELS * cuts[part] - 1, 0)
        hi = LEVELS * cuts[part + 1] - 1
        for f in range(FIELDS):
            copies.append(pltpu.make_async_copy(
                result.at[lo:hi, COLUMNS * f:COLUMNS * (f + 1), :], outs[f].at[lo:hi],
                sem.at[part, f],
            ))
            copies[-1].start()
    for copy in copies:
        copy.wait()


def solution(mesh):
    lon_count, lat_count = mesh.shape["lon"], mesh.shape["lat"]

    def shards(*args):
        levels = args[0].shape[0]
        groups = pl.cdiv(levels, LEVELS)
        chunks = len(cuts_of(groups)) - 1
        f32 = jnp.float32
        vmem = pl.BlockSpec(memory_space=pltpu.VMEM)
        anywhere = pl.BlockSpec(memory_space=pl.ANY)
        y, r = pl.pallas_call(
            functools.partial(halo_and_levels, levels, lon_count, lat_count),
            out_shape=[pltpu.VMEM((groups * LEVELS, ROWS, SPAN), f32)] * 2,
            in_specs=[anywhere] * 7,
            out_specs=[vmem] * 2,
            scratch_shapes=[
                pltpu.VMEM((FIELDS, groups * ROWS, SPAN), f32),
                pltpu.VMEM((FIELDS, groups * ROWS, SPAN), f32),
                pltpu.VMEM((FIELDS, groups * ROWS, SPAN), f32),
                pltpu.VMEM((3, COLUMNS, SPAN), jnp.int32),
                pltpu.VMEM((3, COLUMNS, SPAN), f32),
                pltpu.VMEM((COLUMNS, SPAN), f32),
                pltpu.VMEM((FIELDS, ROWS, SPAN), f32),
                pltpu.VMEM((3, FIELDS, ROWS, SPAN), f32),
                pltpu.VMEM((3, FIELDS, ROWS, SPAN), f32),
                pltpu.VMEM((FIELDS + 1, ROWS, SPAN), f32),
                pltpu.VMEM((FIELDS + 1, ROWS, SPAN), f32),
                pltpu.VMEM((FIELDS + 1, ROWS, SPAN), f32),
                pltpu.SemaphoreType.DMA((8,)),
                pltpu.SemaphoreType.DMA((2, chunks)),
                pltpu.SemaphoreType.DMA((2, chunks)),
                pltpu.SemaphoreType.DMA((2, 2)),
                pltpu.SemaphoreType.DMA((2, 2)),
                pltpu.SemaphoreType.DMA((8,)),
                pltpu.SemaphoreType.DMA((6,)),
            ],
            compiler_params=pltpu.CompilerParams(collective_id=0, has_side_effects=True),
        )(*args)
        return pl.pallas_call(
            functools.partial(substitute, levels),
            out_shape=[jax.ShapeDtypeStruct(args[0].shape, f32)] * FIELDS,
            in_specs=[vmem] * 2,
            out_specs=[anywhere] * FIELDS,
            scratch_shapes=[
                pltpu.VMEM((groups * LEVELS - 1, ROWS, SPAN), f32),
                pltpu.SemaphoreType.DMA((3, FIELDS)),
            ],
        )(*(pltpu.with_memory_space_constraint(q, pltpu.VMEM) for q in (y, r)))

    wide, flat = P(None, "lon", "lat"), P("lon", "lat")
    return jax.shard_map(
        shards,
        mesh=mesh,
        in_specs=(wide,) * 4 + (flat,) * 3,
        out_specs=(wide,) * 4,
        check_vma=False,
    )
```

```python
import functools

import jax
import jax.numpy as jnp
from jax import lax
from jax.experimental import pallas as pl
from jax.experimental.pallas import tpu as pltpu
from jax.sharding import PartitionSpec as P

MESH = pl.DeviceIdType.MESH
DT = 0.05
FIELDS = 4
COLUMNS = 2
SPAN = 128
SEGMENT = 24
LEVELS = 4
ROWS = LEVELS * COLUMNS


def cuts_of(groups):
    return [0, *range(3, groups - 1, 4), groups]


def density(t, s):
    return s * (0.8 + 0.03 * t) - t * (0.2 + 0.05 * t)


def up(x, n):
    return pltpu.roll(x, n % ROWS, 0)


def along(x, n):
    return pltpu.roll(x, n % SPAN, 1)


def halo_and_levels(
    levels, lon_count, lat_count,
    t_in, s_in, u_in, v_in, flooded_in, lateral_in, ambient_in,
    y_out, r_out,
    own, east_tile, west_tile, flooded, lateral, ambient, pack, halo_n, halo_s, rim, rim_x, rim_new,
    local_sem, ew_send, ew_recv, static_send, static_recv, edge_send, edge_recv,
):
    fields_in = (t_in, s_in, u_in, v_in)
    groups = pl.cdiv(levels, LEVELS)
    me = lax.axis_index("lon")
    row = lax.axis_index("lat")
    east = lax.rem(me + 1, lon_count)
    west = lax.rem(me + lon_count - 1, lon_count)
    fold_a = lon_count - 1 - me
    fold_b = lax.rem(2 * lon_count - 2 - me, lon_count)
    top = row == lat_count - 1
    bottom = row == 0
    inner = jnp.logical_not(top)
    above = jnp.logical_not(bottom)
    b_other = jnp.logical_and(top, fold_b != me)
    b_self = jnp.logical_and(top, fold_b == me)
    north = row + 1
    south = row - 1

    barrier = pltpu.get_barrier_semaphore()

    def greet(lon, lat):
        pl.semaphore_signal(barrier, inc=1, device_id=(lon, lat), device_id_type=MESH)

    @pl.when(inner)
    def _():
        greet(me, north)
        greet(west, north)
        greet(east, north)

    @pl.when(above)
    def _():
        greet(me, south)
        greet(west, south)
        greet(east, south)

    greet(west, row)
    greet(east, row)

    @pl.when(top)
    def _():
        greet(fold_a, row)

    @pl.when(b_other)
    def _():
        greet(fold_b, row)

    flat = [x.reshape(levels * COLUMNS, SPAN) for x in fields_in]
    local = [
        pltpu.make_async_copy(flat[f], own.at[f, 0:levels * COLUMNS], local_sem.at[f])
        for f in range(FIELDS)
    ]
    local += [
        pltpu.make_async_copy(flooded_in, flooded.at[0], local_sem.at[4]),
        pltpu.make_async_copy(lateral_in, lateral.at[0], local_sem.at[5]),
        pltpu.make_async_copy(ambient_in, ambient, local_sem.at[6]),
    ]
    for copy in local:
        copy.start()
    for copy in local:
        copy.wait()

    lane = lax.broadcasted_iota(jnp.int32, (ROWS, SPAN), 1)
    sub = lax.broadcasted_iota(jnp.int32, (ROWS, SPAN), 0)
    quad = lane // 4
    place = lane % 4
    tier = sub // COLUMNS
    even = sub % COLUMNS == 0

    def tiled(x):
        return jnp.concatenate([x.astype(jnp.float32)] * LEVELS, axis=0)

    depth_own = tiled(flooded[0])
    mix_own = tiled(lateral[0])
    for f in range(FIELDS):
        def edges(g, acc):
            at = pl.multiple_of(g * ROWS, ROWS)
            return jnp.where(quad == g, pltpu.roll(own[f, pl.ds(at, ROWS)], 4 * g + 2, 1), acc)

        acc = lax.fori_loop(0, groups, edges, jnp.zeros((ROWS, SPAN), jnp.float32), unroll=True)
        if f == 0:
            acc = jnp.where(quad == groups, along(depth_own, 4 * groups + 2), acc)
            acc = jnp.where(quad == groups + 1, along(mix_own, 4 * groups + 6), acc)
        pack[f] = acc

    waits = (
        2 + 3 * inner.astype(jnp.int32) + 3 * above.astype(jnp.int32)
        + top.astype(jnp.int32) + b_other.astype(jnp.int32)
    )
    pl.semaphore_wait(barrier, waits)

    def edge(slot, lon, lat, sent):
        dst = halo_s if slot < 3 else halo_n
        return pltpu.make_async_remote_copy(
            src_ref=pack, dst_ref=dst.at[slot % 3],
            send_sem=edge_send.at[sent], recv_sem=edge_recv.at[slot],
            device_id=(lon, lat), device_id_type=MESH,
        )

    to_a = edge(3, fold_a, row, 6)
    to_b = edge(4, fold_b, row, 7)
    b_copy = pltpu.make_async_copy(pack, halo_n.at[1], local_sem.at[7])
    northward = (edge(0, me, north, 0), edge(1, west, north, 1), edge(2, east, north, 2))
    southward = (edge(3, me, south, 3), edge(4, west, south, 4), edge(5, east, south, 5))

    sides = ((east, west_tile), (west, east_tile))
    statics = [
        [
            pltpu.make_async_remote_copy(
                src_ref=src, dst_ref=dst.at[1 + side],
                send_sem=static_send.at[side, n], recv_sem=static_recv.at[side, n],
                device_id=(lon, row), device_id_type=MESH,
            )
            for n, (src, dst) in enumerate(((flooded_in, flooded), (lateral_in, lateral)))
        ]
        for side, (lon, _) in enumerate(sides)
    ]
    cuts = cuts_of(groups)
    tiles = []
    for c, (first, end) in enumerate(zip(cuts, cuts[1:])):
        lo, hi = first * ROWS, min(end * ROWS, levels * COLUMNS)
        tiles.append([
            pltpu.make_async_remote_copy(
                src_ref=own.at[:, lo:hi], dst_ref=dst.at[:, lo:hi],
                send_sem=ew_send.at[side, c], recv_sem=ew_recv.at[side, c],
                device_id=(lon, row), device_id_type=MESH,
            )
            for side, (lon, dst) in enumerate(sides)
        ])

    eastward, westward = 0, 1

    def send_tiles(side, chunks):
        for c in chunks:
            tiles[c][side].start()

    @pl.when(top)
    def _():
        to_a.start()

    @pl.when(b_other)
    def _():
        to_b.start()

    @pl.when(b_self)
    def _():
        b_copy.start()

    @pl.when(inner)
    def _():
        northward[2].start()

    @pl.when(above)
    def _():
        southward[2].start()

    for copy in statics[eastward]:
        copy.start()
    run_last = lax.rem(me, SEGMENT) == SEGMENT - 1

    @pl.when(run_last)
    def _():
        send_tiles(eastward, range(len(tiles)))

    @pl.when(inner)
    def _():
        northward[0].start()
        northward[1].start()

    @pl.when(above)
    def _():
        southward[0].start()
        southward[1].start()

    @pl.when(jnp.logical_not(run_last))
    def _():
        send_tiles(eastward, range(len(tiles)))

    for copy in statics[westward]:
        copy.start()
    send_tiles(westward, range(len(tiles)))

    def prefix(d):
        two = up(d, COLUMNS)
        s = d + jnp.where(tier >= 1, two, 0.0)
        pair = d + two
        return s + jnp.where(tier >= 2, up(s, 2 * COLUMNS), 0.0), pair + up(pair, 2 * COLUMNS)

    def packed_pressure(t, s):
        inside, total = prefix((0.25 * DT) * density(t, s))
        for n in (4, 8, 16, 32, 64):
            total = total + jnp.where(lane >= n, along(total, n), 0.0)
        return inside + jnp.where(lane >= 4, along(total, 4), 0.0)

    def every_quad(x, n):
        x = jnp.where(quad == n, x, 0.0)
        for n in (4, 8, 16, 32, 64):
            x = x + along(x, n)
        return x

    own_edge = [pack[f] for f in range(FIELDS)]
    o_depth, o_mix = every_quad(own_edge[0], groups), (0.5 * DT) * every_quad(own_edge[0], groups + 1)
    own_edge.append(packed_pressure(own_edge[0], own_edge[1]))

    for side in statics:
        for copy in side:
            copy.wait_recv()

    @pl.when(above)
    def _():
        for copy in northward:
            copy.wait_recv()

    @pl.when(inner)
    def _():
        for copy in southward:
            copy.wait_recv()

    @pl.when(top)
    def _():
        to_a.wait_recv()

    @pl.when(b_other)
    def _():
        to_b.wait_recv()

    @pl.when(b_self)
    def _():
        b_copy.wait()

    def sideways(o, x):
        return jnp.where(even, up(o, -1), up(x, 1)), jnp.where(even, up(x, -1), up(o, 1))

    for f in range(FIELDS):
        sign = 1.0 if f < 2 else -1.0
        n0, n1, n2 = halo_n[0, f], halo_n[1, f], halo_n[2, f]
        s0, s1, s2 = halo_s[0, f], halo_s[1, f], halo_s[2, f]
        for dst, n, s, fold in (
            (rim, n0, s0, jnp.where(even, n0, n1)),
            (rim_x, jnp.where(even, n1, n2), jnp.where(even, s1, s2), jnp.where(even, n1, n0)),
        ):
            n = jnp.where(place == 1, along(n, -1), along(n, -3))
            n = jnp.where(top, sign * fold, n)
            s = jnp.where(place == 2, along(s, 1), along(s, 3))
            s = jnp.where(bottom, 0.0, s)
            dst[f] = jnp.where(place < 2, n, s)

    def turning(j):
        total = lat_count * SPAN
        m = jnp.where(j >= total, 2 * total - 1 - j, j)
        return DT * (0.2 + m.astype(jnp.float32) / total)

    def faces(depth, mix, sides_of):
        return [(jnp.minimum(depth, d), mix + m) for d, m in zip(sides_of(0), sides_of(1))]

    def weights(level, depth, around):
        c = [jnp.where(level < d, m, 0.0) for d, m in around]
        return c, 1.0 - ((c[0] + c[1]) + (c[2] + c[3])), level < depth

    def update(weight, turn, cells, e, w, n, s):
        (ce, cw, cn, cs), keep, wet = weight
        half_u = (0.5 * DT) * cells[2]
        half_v = (0.5 * DT) * cells[3]
        ce, cw, cn, cs = ce - half_u, cw + half_u, cn - half_v, cs + half_v
        out = []
        for f in range(FIELDS):
            x = (keep * cells[f] + ce * e[f]) + (cw * w[f] + (cn * n[f] + cs * s[f]))
            if f == 2:
                x = x + (turn * cells[3] - (e[4] - w[4]))
            if f == 3:
                x = x - (turn * cells[2] + (n[4] - s[4]))
            out.append(jnp.where(wet, x, 0.0))
        return out

    cells = [rim[f] for f in range(FIELDS)]
    cells_x = [rim_x[f] for f in range(FIELDS)]
    rim_depth, rim_mix = every_quad(cells[0], groups), (0.5 * DT) * every_quad(cells[0], groups + 1)
    x_depth, x_mix = every_quad(cells_x[0], groups), (0.5 * DT) * every_quad(cells_x[0], groups + 1)
    for block in (cells, cells_x):
        block.append(packed_pressure(block[0], block[1]))
    rim[4] = cells[4]
    rim_x[4] = cells_x[4]

    def around_rim(c, x, o):
        e, w = sideways(c, x)
        return e, w, jnp.where(place == 1, along(c, 1), o), jnp.where(place == 2, along(c, -1), o)

    around = [around_rim(*q) for q in zip(cells, cells_x, own_edge)]
    statics_around = (around_rim(rim_depth, x_depth, o_depth), around_rim(rim_mix, x_mix, o_mix))
    rim_level = (LEVELS * quad + tier).astype(jnp.float32)
    rim_row = jnp.where(place < 2, (row + 1) * SPAN + 1 - place, row * SPAN + 1 - place)
    new = update(
        weights(rim_level, rim_depth, faces(rim_depth, rim_mix, lambda n: statics_around[n])),
        turning(rim_row), cells, *[[q[n] for q in around] for n in range(4)],
    )
    new.append(packed_pressure(new[0], new[1]))
    for q in range(FIELDS + 1):
        rim_new[q] = new[q]

    first_lane = lane == 0
    last_lane = lane == SPAN - 1

    def beside(x, r):
        return jnp.where(last_lane, r, along(x, -1)), jnp.where(first_lane, r, along(x, 1))

    def shifted(x, g):
        return pltpu.roll(x, lax.rem(2 * SPAN - 2 - 4 * g, SPAN) if not isinstance(g, int) else (-2 - 4 * g) % SPAN, 1)

    def around_own(o, x, r):
        return sideways(o, x) + beside(o, r)

    def around_x(o, x, z, r):
        return (jnp.where(even, z, up(o, 1)), jnp.where(even, up(o, -1), z)) + beside(x, r)

    def split(e, w):
        return jnp.where(even, e, w), jnp.where(even, up(e, -1), up(w, 1))

    depth_x, depth_z = split(tiled(flooded[2]), tiled(flooded[1]))
    mix_x, mix_z = split(tiled(lateral[2]), tiled(lateral[1]))
    mix_o, mix_x, mix_z = ((0.5 * DT) * x for x in (mix_own, mix_x, mix_z))
    rim_depth_at, rim_mix_at = shifted(rim_depth, 0), shifted(rim_mix, 0)
    x_depth_at, x_mix_at = shifted(x_depth, 0), shifted(x_mix, 0)
    own_statics = (around_own(depth_own, depth_x, rim_depth_at), around_own(mix_o, mix_x, rim_mix_at))
    x_statics = (
        around_x(depth_own, depth_x, depth_z, x_depth_at), around_x(mix_o, mix_x, mix_z, x_mix_at)
    )
    own_faces = faces(depth_own, mix_o, lambda n: own_statics[n])
    x_faces = faces(depth_x, mix_x, lambda n: x_statics[n])
    turn = turning(row * SPAN + lane)
    ambient_all = tiled(ambient[...])
    tier_level = tier.astype(jnp.float32)
    low = tier % 2 == 0
    lower_half = tier < 2

    def per_level(blocks):
        a, b, c, d = blocks
        ab0, ab1 = jnp.where(low, a, up(b, 2)), jnp.where(low, up(a, -2), b)
        cd0, cd1 = jnp.where(low, c, up(d, 2)), jnp.where(low, up(c, -2), d)
        return (
            jnp.where(lower_half, ab0, up(cd0, 4)), jnp.where(lower_half, ab1, up(cd1, 4)),
            jnp.where(lower_half, up(ab0, 4), cd0), jnp.where(lower_half, up(ab1, 4), cd1),
        )

    def repeated(a):
        ab0, ab1 = jnp.where(low, a, up(a, 2)), jnp.where(low, up(a, -2), a)
        r0, r1 = up(ab0, 4), up(ab1, 4)
        return (
            jnp.where(lower_half, ab0, r0), jnp.where(lower_half, ab1, r1),
            jnp.where(lower_half, r0, ab0), jnp.where(lower_half, r1, ab1),
        )

    def step(g, carry):
        po, px, pz, p2o, p2x, heavy, held, lower, inverse, value = carry
        at = pl.multiple_of(g * ROWS, ROWS)
        o = [own[f, pl.ds(at, ROWS)] for f in range(FIELDS)]
        xz = [split(east_tile[f, pl.ds(at, ROWS)], west_tile[f, pl.ds(at, ROWS)]) for f in range(FIELDS)]
        x, z = [q[0] for q in xz], [q[1] for q in xz]
        pressures = []
        for block, total in ((o, po), (x, px), (z, pz)):
            inside, more = prefix((0.25 * DT) * density(block[0], block[1]))
            block.append(inside + total)
            pressures.append(total + more)
        level = tier_level + (LEVELS * g).astype(jnp.float32)
        around = [around_own(*q, shifted(rim[n], g)) for n, q in enumerate(zip(o, x))]
        weight = weights(level, depth_own, own_faces)
        o2 = update(weight, turn, o, *[[q[n] for q in around] for n in range(4)])
        around = [around_x(*q, shifted(rim_x[n], g)) for n, q in enumerate(zip(o, x, z))]
        x2 = update(
            weights(level, depth_x, x_faces), turn, x, *[[q[n] for q in around] for n in range(4)]
        )
        for block, total in ((o2, p2o), (x2, p2x)):
            inside, more = prefix((0.25 * DT) * density(block[0], block[1]))
            block.append(inside + total)
            pressures.append(total + more)
        around = [around_own(*q, shifted(rim_new[n], g)) for n, q in enumerate(zip(o2, x2))]
        done = update(weight, turn, o2, *[[q[n] for q in around] for n in range(4)])

        weighed = density(done[0], done[1])
        new_heavy = up(weighed, COLUMNS)
        rise = weighed - jnp.where(tier == 0, heavy, new_heavy)
        a = ambient_all * (0.2 + 1.0 / (1.0 + 10.0 * jnp.maximum(rise, 0.0)))
        a = jnp.where(jnp.logical_and(weight[2], level > 0.5), a, 0.0)
        uppers = repeated(a)
        fields = per_level(done)
        xs = (held,) + fields[:3]
        lowers = (lower,) + uppers[:3]
        dets = []
        last, before = None, inverse
        for n in range(LEVELS):
            main = 1.0 + (lowers[n] + uppers[n])
            square = lowers[n] * lowers[n]
            if n == 0:
                det = main - square * before
            elif n == 1:
                det = main * last - square
            else:
                det = main * last - square * before
            dets.append(det)
            last, before = det, last
        ys, rs = [], []
        for n in range(LEVELS):
            inverse = 1.0 / dets[n]
            if n > 0:
                inverse = inverse * dets[n - 1]
            value = (xs[n] + lowers[n] * value) * inverse
            ys.append(value)
            rs.append(uppers[n] * inverse)
        y, r = ys[-1], rs[-1]
        for n in range(LEVELS - 1, -1, -1):
            if n < LEVELS - 1:
                y, r = ys[n] + rs[n] * y, rs[n] * r
            y_out[LEVELS * g + n] = y
            r_out[LEVELS * g + n] = r
        return (*pressures, new_heavy, fields[3], uppers[3], inverse, value)

    zero = jnp.zeros((ROWS, SPAN), jnp.float32)
    carry = (zero,) * 8 + (zero + 1.0, zero)
    for c, (first, end) in enumerate(zip(cuts, cuts[1:])):
        for copy in tiles[c]:
            copy.wait_recv()
        carry = lax.fori_loop(first, end, step, carry, unroll=2)

    for part in (*tiles, *statics):
        for copy in part:
            copy.wait_send()

    @pl.when(top)
    def _():
        to_a.wait_send()

    @pl.when(b_other)
    def _():
        to_b.wait_send()

    @pl.when(inner)
    def _():
        for copy in northward:
            copy.wait_send()

    @pl.when(above)
    def _():
        for copy in southward:
            copy.wait_send()


def substitute(levels, y, r, t_out, s_out, u_out, v_out, result, sem):
    outs = (t_out, s_out, u_out, v_out)
    groups = pl.cdiv(levels, LEVELS)
    cuts = [0, groups // 3, 2 * groups // 3, groups]
    copies = []
    below = jnp.zeros((ROWS, SPAN), jnp.float32)
    for part in range(len(cuts) - 2, -1, -1):
        for g in range(cuts[part + 1] - 1, cuts[part] - 1, -1):
            at = LEVELS * g
            rows = [y[at + n] + r[at + n] * below for n in range(LEVELS)]
            below = rows[0]
            for n in range(LEVELS):
                if at + n > 0:
                    result[at + n - 1] = rows[n]
        lo = max(LEVELS * cuts[part] - 1, 0)
        hi = LEVELS * cuts[part + 1] - 1
        for f in range(FIELDS):
            copies.append(pltpu.make_async_copy(
                result.at[lo:hi, COLUMNS * f:COLUMNS * (f + 1), :], outs[f].at[lo:hi],
                sem.at[part, f],
            ))
            copies[-1].start()
    for copy in copies:
        copy.wait()


def solution(mesh):
    lon_count, lat_count = mesh.shape["lon"], mesh.shape["lat"]

    def shards(*args):
        levels = args[0].shape[0]
        groups = pl.cdiv(levels, LEVELS)
        chunks = len(cuts_of(groups)) - 1
        f32 = jnp.float32
        vmem = pl.BlockSpec(memory_space=pltpu.VMEM)
        anywhere = pl.BlockSpec(memory_space=pl.ANY)
        y, r = pl.pallas_call(
            functools.partial(halo_and_levels, levels, lon_count, lat_count),
            out_shape=[pltpu.VMEM((groups * LEVELS, ROWS, SPAN), f32)] * 2,
            in_specs=[anywhere] * 7,
            out_specs=[vmem] * 2,
            scratch_shapes=[
                pltpu.VMEM((FIELDS, groups * ROWS, SPAN), f32),
                pltpu.VMEM((FIELDS, groups * ROWS, SPAN), f32),
                pltpu.VMEM((FIELDS, groups * ROWS, SPAN), f32),
                pltpu.VMEM((3, COLUMNS, SPAN), jnp.int32),
                pltpu.VMEM((3, COLUMNS, SPAN), f32),
                pltpu.VMEM((COLUMNS, SPAN), f32),
                pltpu.VMEM((FIELDS, ROWS, SPAN), f32),
                pltpu.VMEM((3, FIELDS, ROWS, SPAN), f32),
                pltpu.VMEM((3, FIELDS, ROWS, SPAN), f32),
                pltpu.VMEM((FIELDS + 1, ROWS, SPAN), f32),
                pltpu.VMEM((FIELDS + 1, ROWS, SPAN), f32),
                pltpu.VMEM((FIELDS + 1, ROWS, SPAN), f32),
                pltpu.SemaphoreType.DMA((8,)),
                pltpu.SemaphoreType.DMA((2, chunks)),
                pltpu.SemaphoreType.DMA((2, chunks)),
                pltpu.SemaphoreType.DMA((2, 2)),
                pltpu.SemaphoreType.DMA((2, 2)),
                pltpu.SemaphoreType.DMA((8,)),
                pltpu.SemaphoreType.DMA((6,)),
            ],
            compiler_params=pltpu.CompilerParams(collective_id=0, has_side_effects=True),
        )(*args)
        return pl.pallas_call(
            functools.partial(substitute, levels),
            out_shape=[jax.ShapeDtypeStruct(args[0].shape, f32)] * FIELDS,
            in_specs=[vmem] * 2,
            out_specs=[anywhere] * FIELDS,
            scratch_shapes=[
                pltpu.VMEM((groups * LEVELS - 1, ROWS, SPAN), f32),
                pltpu.SemaphoreType.DMA((3, FIELDS)),
            ],
        )(*(pltpu.with_memory_space_constraint(q, pltpu.VMEM) for q in (y, r)))

    wide, flat = P(None, "lon", "lat"), P("lon", "lat")
    return jax.shard_map(
        shards,
        mesh=mesh,
        in_specs=(wide,) * 4 + (flat,) * 3,
        out_specs=(wide,) * 4,
        check_vma=False,
    )
```

```python
import functools

import jax
import jax.numpy as jnp
from jax import lax
from jax.experimental import pallas as pl
from jax.experimental.pallas import tpu as pltpu
from jax.sharding import PartitionSpec as P

MESH = pl.DeviceIdType.MESH
DT = 0.05
FIELDS = 4
COLUMNS = 2
SPAN = 128
SEGMENT = 24
LEVELS = 4
ROWS = LEVELS * COLUMNS


def cuts_of(groups):
    return [0, *range(5, groups - 1, 6), groups]


def density(t, s):
    return s * (0.8 + 0.03 * t) - t * (0.2 + 0.05 * t)


def up(x, n):
    return pltpu.roll(x, n % ROWS, 0)


def along(x, n):
    return pltpu.roll(x, n % SPAN, 1)


def halo_and_levels(
    levels, lon_count, lat_count,
    t_in, s_in, u_in, v_in, flooded_in, lateral_in, ambient_in,
    y_out, r_out,
    own, east_tile, west_tile, flooded, lateral, ambient, pack, halo_n, halo_s, rim, rim_x, rim_new,
    local_sem, ew_send, ew_recv, static_send, static_recv, edge_send, edge_recv,
):
    fields_in = (t_in, s_in, u_in, v_in)
    groups = pl.cdiv(levels, LEVELS)
    me = lax.axis_index("lon")
    row = lax.axis_index("lat")
    east = lax.rem(me + 1, lon_count)
    west = lax.rem(me + lon_count - 1, lon_count)
    fold_a = lon_count - 1 - me
    fold_b = lax.rem(2 * lon_count - 2 - me, lon_count)
    top = row == lat_count - 1
    bottom = row == 0
    inner = jnp.logical_not(top)
    above = jnp.logical_not(bottom)
    b_other = jnp.logical_and(top, fold_b != me)
    b_self = jnp.logical_and(top, fold_b == me)
    north = row + 1
    south = row - 1

    barrier = pltpu.get_barrier_semaphore()

    def greet(lon, lat):
        pl.semaphore_signal(barrier, inc=1, device_id=(lon, lat), device_id_type=MESH)

    @pl.when(inner)
    def _():
        greet(me, north)
        greet(west, north)
        greet(east, north)

    @pl.when(above)
    def _():
        greet(me, south)
        greet(west, south)
        greet(east, south)

    greet(west, row)
    greet(east, row)

    @pl.when(top)
    def _():
        greet(fold_a, row)

    @pl.when(b_other)
    def _():
        greet(fold_b, row)

    flat = [x.reshape(levels * COLUMNS, SPAN) for x in fields_in]
    local = [
        pltpu.make_async_copy(flat[f], own.at[f, 0:levels * COLUMNS], local_sem.at[f])
        for f in range(FIELDS)
    ]
    local += [
        pltpu.make_async_copy(flooded_in, flooded.at[0], local_sem.at[4]),
        pltpu.make_async_copy(lateral_in, lateral.at[0], local_sem.at[5]),
        pltpu.make_async_copy(ambient_in, ambient, local_sem.at[6]),
    ]
    for copy in local:
        copy.start()
    for copy in local:
        copy.wait()

    lane = lax.broadcasted_iota(jnp.int32, (ROWS, SPAN), 1)
    sub = lax.broadcasted_iota(jnp.int32, (ROWS, SPAN), 0)
    quad = lane // 4
    place = lane % 4
    tier = sub // COLUMNS
    even = sub % COLUMNS == 0

    def tiled(x):
        return jnp.concatenate([x.astype(jnp.float32)] * LEVELS, axis=0)

    depth_own = tiled(flooded[0])
    mix_own = tiled(lateral[0])
    for f in range(FIELDS):
        def edges(g, acc):
            at = pl.multiple_of(g * ROWS, ROWS)
            return jnp.where(quad == g, pltpu.roll(own[f, pl.ds(at, ROWS)], 4 * g + 2, 1), acc)

        acc = lax.fori_loop(0, groups, edges, jnp.zeros((ROWS, SPAN), jnp.float32), unroll=True)
        if f == 0:
            acc = jnp.where(quad == groups, along(depth_own, 4 * groups + 2), acc)
            acc = jnp.where(quad == groups + 1, along(mix_own, 4 * groups + 6), acc)
        pack[f] = acc

    waits = (
        2 + 3 * inner.astype(jnp.int32) + 3 * above.astype(jnp.int32)
        + top.astype(jnp.int32) + b_other.astype(jnp.int32)
    )
    pl.semaphore_wait(barrier, waits)

    def edge(slot, lon, lat, sent):
        dst = halo_s if slot < 3 else halo_n
        return pltpu.make_async_remote_copy(
            src_ref=pack, dst_ref=dst.at[slot % 3],
            send_sem=edge_send.at[sent], recv_sem=edge_recv.at[slot],
            device_id=(lon, lat), device_id_type=MESH,
        )

    to_a = edge(3, fold_a, row, 6)
    to_b = edge(4, fold_b, row, 7)
    b_copy = pltpu.make_async_copy(pack, halo_n.at[1], local_sem.at[7])
    northward = (edge(0, me, north, 0), edge(1, west, north, 1), edge(2, east, north, 2))
    southward = (edge(3, me, south, 3), edge(4, west, south, 4), edge(5, east, south, 5))

    sides = ((east, west_tile), (west, east_tile))
    statics = [
        [
            pltpu.make_async_remote_copy(
                src_ref=src, dst_ref=dst.at[1 + side],
                send_sem=static_send.at[side, n], recv_sem=static_recv.at[side, n],
                device_id=(lon, row), device_id_type=MESH,
            )
            for n, (src, dst) in enumerate(((flooded_in, flooded), (lateral_in, lateral)))
        ]
        for side, (lon, _) in enumerate(sides)
    ]
    cuts = cuts_of(groups)
    tiles = []
    for c, (first, end) in enumerate(zip(cuts, cuts[1:])):
        lo, hi = first * ROWS, min(end * ROWS, levels * COLUMNS)
        tiles.append([
            pltpu.make_async_remote_copy(
                src_ref=own.at[:, lo:hi], dst_ref=dst.at[:, lo:hi],
                send_sem=ew_send.at[side, c], recv_sem=ew_recv.at[side, c],
                device_id=(lon, row), device_id_type=MESH,
            )
            for side, (lon, dst) in enumerate(sides)
        ])

    eastward, westward = 0, 1

    def send_tiles(side, chunks):
        for c in chunks:
            tiles[c][side].start()

    @pl.when(top)
    def _():
        to_a.start()

    @pl.when(b_other)
    def _():
        to_b.start()

    @pl.when(b_self)
    def _():
        b_copy.start()

    @pl.when(inner)
    def _():
        northward[2].start()

    @pl.when(above)
    def _():
        southward[2].start()

    for copy in statics[eastward]:
        copy.start()
    run_last = lax.rem(me, SEGMENT) == SEGMENT - 1

    @pl.when(run_last)
    def _():
        send_tiles(eastward, range(len(tiles)))

    @pl.when(inner)
    def _():
        northward[0].start()
        northward[1].start()

    @pl.when(above)
    def _():
        southward[0].start()
        southward[1].start()

    @pl.when(jnp.logical_not(run_last))
    def _():
        send_tiles(eastward, range(len(tiles)))

    for copy in statics[westward]:
        copy.start()
    send_tiles(westward, range(len(tiles)))

    def prefix(d):
        two = up(d, COLUMNS)
        s = d + jnp.where(tier >= 1, two, 0.0)
        pair = d + two
        return s + jnp.where(tier >= 2, up(s, 2 * COLUMNS), 0.0), pair + up(pair, 2 * COLUMNS)

    def packed_pressure(t, s):
        inside, total = prefix((0.25 * DT) * density(t, s))
        for n in (4, 8, 16, 32, 64):
            total = total + jnp.where(lane >= n, along(total, n), 0.0)
        return inside + jnp.where(lane >= 4, along(total, 4), 0.0)

    def every_quad(x, n):
        x = jnp.where(quad == n, x, 0.0)
        for n in (4, 8, 16, 32, 64):
            x = x + along(x, n)
        return x

    own_edge = [pack[f] for f in range(FIELDS)]
    o_depth, o_mix = every_quad(own_edge[0], groups), (0.5 * DT) * every_quad(own_edge[0], groups + 1)
    own_edge.append(packed_pressure(own_edge[0], own_edge[1]))

    for side in statics:
        for copy in side:
            copy.wait_recv()

    @pl.when(above)
    def _():
        for copy in northward:
            copy.wait_recv()

    @pl.when(inner)
    def _():
        for copy in southward:
            copy.wait_recv()

    @pl.when(top)
    def _():
        to_a.wait_recv()

    @pl.when(b_other)
    def _():
        to_b.wait_recv()

    @pl.when(b_self)
    def _():
        b_copy.wait()

    def sideways(o, x):
        return jnp.where(even, up(o, -1), up(x, 1)), jnp.where(even, up(x, -1), up(o, 1))

    for f in range(FIELDS):
        sign = 1.0 if f < 2 else -1.0
        n0, n1, n2 = halo_n[0, f], halo_n[1, f], halo_n[2, f]
        s0, s1, s2 = halo_s[0, f], halo_s[1, f], halo_s[2, f]
        for dst, n, s, fold in (
            (rim, n0, s0, jnp.where(even, n0, n1)),
            (rim_x, jnp.where(even, n1, n2), jnp.where(even, s1, s2), jnp.where(even, n1, n0)),
        ):
            n = jnp.where(place == 1, along(n, -1), along(n, -3))
            n = jnp.where(top, sign * fold, n)
            s = jnp.where(place == 2, along(s, 1), along(s, 3))
            s = jnp.where(bottom, 0.0, s)
            dst[f] = jnp.where(place < 2, n, s)

    def turning(j):
        total = lat_count * SPAN
        m = jnp.where(j >= total, 2 * total - 1 - j, j)
        return DT * (0.2 + m.astype(jnp.float32) / total)

    def faces(depth, mix, sides_of):
        return [(jnp.minimum(depth, d), mix + m) for d, m in zip(sides_of(0), sides_of(1))]

    def weights(level, depth, around):
        c = [jnp.where(level < d, m, 0.0) for d, m in around]
        return c, 1.0 - ((c[0] + c[1]) + (c[2] + c[3])), level < depth

    def update(weight, turn, cells, e, w, n, s):
        (ce, cw, cn, cs), keep, wet = weight
        half_u = (0.5 * DT) * cells[2]
        half_v = (0.5 * DT) * cells[3]
        ce, cw, cn, cs = ce - half_u, cw + half_u, cn - half_v, cs + half_v
        out = []
        for f in range(FIELDS):
            x = (keep * cells[f] + ce * e[f]) + (cw * w[f] + (cn * n[f] + cs * s[f]))
            if f == 2:
                x = x + (turn * cells[3] - (e[4] - w[4]))
            if f == 3:
                x = x - (turn * cells[2] + (n[4] - s[4]))
            out.append(jnp.where(wet, x, 0.0))
        return out

    cells = [rim[f] for f in range(FIELDS)]
    cells_x = [rim_x[f] for f in range(FIELDS)]
    rim_depth, rim_mix = every_quad(cells[0], groups), (0.5 * DT) * every_quad(cells[0], groups + 1)
    x_depth, x_mix = every_quad(cells_x[0], groups), (0.5 * DT) * every_quad(cells_x[0], groups + 1)
    for block in (cells, cells_x):
        block.append(packed_pressure(block[0], block[1]))
    rim[4] = cells[4]
    rim_x[4] = cells_x[4]

    def around_rim(c, x, o):
        e, w = sideways(c, x)
        return e, w, jnp.where(place == 1, along(c, 1), o), jnp.where(place == 2, along(c, -1), o)

    around = [around_rim(*q) for q in zip(cells, cells_x, own_edge)]
    statics_around = (around_rim(rim_depth, x_depth, o_depth), around_rim(rim_mix, x_mix, o_mix))
    rim_level = (LEVELS * quad + tier).astype(jnp.float32)
    rim_row = jnp.where(place < 2, (row + 1) * SPAN + 1 - place, row * SPAN + 1 - place)
    new = update(
        weights(rim_level, rim_depth, faces(rim_depth, rim_mix, lambda n: statics_around[n])),
        turning(rim_row), cells, *[[q[n] for q in around] for n in range(4)],
    )
    new.append(packed_pressure(new[0], new[1]))
    for q in range(FIELDS + 1):
        rim_new[q] = new[q]

    first_lane = lane == 0
    last_lane = lane == SPAN - 1

    def beside(x, r):
        return jnp.where(last_lane, r, along(x, -1)), jnp.where(first_lane, r, along(x, 1))

    def shifted(x, g):
        return pltpu.roll(x, lax.rem(2 * SPAN - 2 - 4 * g, SPAN) if not isinstance(g, int) else (-2 - 4 * g) % SPAN, 1)

    def around_own(o, x, r):
        return sideways(o, x) + beside(o, r)

    def around_x(o, x, z, r):
        return (jnp.where(even, z, up(o, 1)), jnp.where(even, up(o, -1), z)) + beside(x, r)

    def split(e, w):
        return jnp.where(even, e, w), jnp.where(even, up(e, -1), up(w, 1))

    depth_x, depth_z = split(tiled(flooded[2]), tiled(flooded[1]))
    mix_x, mix_z = split(tiled(lateral[2]), tiled(lateral[1]))
    mix_o, mix_x, mix_z = ((0.5 * DT) * x for x in (mix_own, mix_x, mix_z))
    rim_depth_at, rim_mix_at = shifted(rim_depth, 0), shifted(rim_mix, 0)
    x_depth_at, x_mix_at = shifted(x_depth, 0), shifted(x_mix, 0)
    own_statics = (around_own(depth_own, depth_x, rim_depth_at), around_own(mix_o, mix_x, rim_mix_at))
    x_statics = (
        around_x(depth_own, depth_x, depth_z, x_depth_at), around_x(mix_o, mix_x, mix_z, x_mix_at)
    )
    own_faces = faces(depth_own, mix_o, lambda n: own_statics[n])
    x_faces = faces(depth_x, mix_x, lambda n: x_statics[n])
    turn = turning(row * SPAN + lane)
    ambient_all = tiled(ambient[...])
    tier_level = tier.astype(jnp.float32)
    low = tier % 2 == 0
    lower_half = tier < 2

    def per_level(blocks):
        a, b, c, d = blocks
        ab0, ab1 = jnp.where(low, a, up(b, 2)), jnp.where(low, up(a, -2), b)
        cd0, cd1 = jnp.where(low, c, up(d, 2)), jnp.where(low, up(c, -2), d)
        return (
            jnp.where(lower_half, ab0, up(cd0, 4)), jnp.where(lower_half, ab1, up(cd1, 4)),
            jnp.where(lower_half, up(ab0, 4), cd0), jnp.where(lower_half, up(ab1, 4), cd1),
        )

    def repeated(a):
        ab0, ab1 = jnp.where(low, a, up(a, 2)), jnp.where(low, up(a, -2), a)
        r0, r1 = up(ab0, 4), up(ab1, 4)
        return (
            jnp.where(lower_half, ab0, r0), jnp.where(lower_half, ab1, r1),
            jnp.where(lower_half, r0, ab0), jnp.where(lower_half, r1, ab1),
        )

    def step(g, carry):
        po, px, pz, p2o, p2x, heavy, held, lower, inverse, value = carry
        at = pl.multiple_of(g * ROWS, ROWS)
        o = [own[f, pl.ds(at, ROWS)] for f in range(FIELDS)]
        xz = [split(east_tile[f, pl.ds(at, ROWS)], west_tile[f, pl.ds(at, ROWS)]) for f in range(FIELDS)]
        x, z = [q[0] for q in xz], [q[1] for q in xz]
        pressures = []
        for block, total in ((o, po), (x, px), (z, pz)):
            inside, more = prefix((0.25 * DT) * density(block[0], block[1]))
            block.append(inside + total)
            pressures.append(total + more)
        level = tier_level + (LEVELS * g).astype(jnp.float32)
        around = [around_own(*q, shifted(rim[n], g)) for n, q in enumerate(zip(o, x))]
        weight = weights(level, depth_own, own_faces)
        o2 = update(weight, turn, o, *[[q[n] for q in around] for n in range(4)])
        around = [around_x(*q, shifted(rim_x[n], g)) for n, q in enumerate(zip(o, x, z))]
        x2 = update(
            weights(level, depth_x, x_faces), turn, x, *[[q[n] for q in around] for n in range(4)]
        )
        for block, total in ((o2, p2o), (x2, p2x)):
            inside, more = prefix((0.25 * DT) * density(block[0], block[1]))
            block.append(inside + total)
            pressures.append(total + more)
        around = [around_own(*q, shifted(rim_new[n], g)) for n, q in enumerate(zip(o2, x2))]
        done = update(weight, turn, o2, *[[q[n] for q in around] for n in range(4)])

        weighed = density(done[0], done[1])
        new_heavy = up(weighed, COLUMNS)
        rise = weighed - jnp.where(tier == 0, heavy, new_heavy)
        a = ambient_all * (0.2 + 1.0 / (1.0 + 10.0 * jnp.maximum(rise, 0.0)))
        a = jnp.where(jnp.logical_and(weight[2], level > 0.5), a, 0.0)
        uppers = repeated(a)
        fields = per_level(done)
        xs = (held,) + fields[:3]
        lowers = (lower,) + uppers[:3]
        dets = []
        last, before = None, inverse
        for n in range(LEVELS):
            main = 1.0 + (lowers[n] + uppers[n])
            square = lowers[n] * lowers[n]
            if n == 0:
                det = main - square * before
            elif n == 1:
                det = main * last - square
            else:
                det = main * last - square * before
            dets.append(det)
            last, before = det, last
        ys, rs = [], []
        for n in range(LEVELS):
            inverse = 1.0 / dets[n]
            if n > 0:
                inverse = inverse * dets[n - 1]
            value = (xs[n] + lowers[n] * value) * inverse
            ys.append(value)
            rs.append(uppers[n] * inverse)
        y, r = ys[-1], rs[-1]
        for n in range(LEVELS - 1, -1, -1):
            if n < LEVELS - 1:
                y, r = ys[n] + rs[n] * y, rs[n] * r
            y_out[LEVELS * g + n] = y
            r_out[LEVELS * g + n] = r
        return (*pressures, new_heavy, fields[3], uppers[3], inverse, value)

    zero = jnp.zeros((ROWS, SPAN), jnp.float32)
    carry = (zero,) * 8 + (zero + 1.0, zero)
    for c, (first, end) in enumerate(zip(cuts, cuts[1:])):
        for copy in tiles[c]:
            copy.wait_recv()
        carry = lax.fori_loop(first, end, step, carry, unroll=2)

    for part in (*tiles, *statics):
        for copy in part:
            copy.wait_send()

    @pl.when(top)
    def _():
        to_a.wait_send()

    @pl.when(b_other)
    def _():
        to_b.wait_send()

    @pl.when(inner)
    def _():
        for copy in northward:
            copy.wait_send()

    @pl.when(above)
    def _():
        for copy in southward:
            copy.wait_send()


def substitute(levels, y, r, t_out, s_out, u_out, v_out, result, sem):
    outs = (t_out, s_out, u_out, v_out)
    groups = pl.cdiv(levels, LEVELS)
    cuts = [0, groups // 3, 2 * groups // 3, groups]
    copies = []
    below = jnp.zeros((ROWS, SPAN), jnp.float32)
    for part in range(len(cuts) - 2, -1, -1):
        for g in range(cuts[part + 1] - 1, cuts[part] - 1, -1):
            at = LEVELS * g
            rows = [y[at + n] + r[at + n] * below for n in range(LEVELS)]
            below = rows[0]
            for n in range(LEVELS):
                if at + n > 0:
                    result[at + n - 1] = rows[n]
        lo = max(LEVELS * cuts[part] - 1, 0)
        hi = LEVELS * cuts[part + 1] - 1
        for f in range(FIELDS):
            copies.append(pltpu.make_async_copy(
                result.at[lo:hi, COLUMNS * f:COLUMNS * (f + 1), :], outs[f].at[lo:hi],
                sem.at[part, f],
            ))
            copies[-1].start()
    for copy in copies:
        copy.wait()


def solution(mesh):
    lon_count, lat_count = mesh.shape["lon"], mesh.shape["lat"]

    def shards(*args):
        levels = args[0].shape[0]
        groups = pl.cdiv(levels, LEVELS)
        chunks = len(cuts_of(groups)) - 1
        f32 = jnp.float32
        vmem = pl.BlockSpec(memory_space=pltpu.VMEM)
        anywhere = pl.BlockSpec(memory_space=pl.ANY)
        y, r = pl.pallas_call(
            functools.partial(halo_and_levels, levels, lon_count, lat_count),
            out_shape=[pltpu.VMEM((groups * LEVELS, ROWS, SPAN), f32)] * 2,
            in_specs=[anywhere] * 7,
            out_specs=[vmem] * 2,
            scratch_shapes=[
                pltpu.VMEM((FIELDS, groups * ROWS, SPAN), f32),
                pltpu.VMEM((FIELDS, groups * ROWS, SPAN), f32),
                pltpu.VMEM((FIELDS, groups * ROWS, SPAN), f32),
                pltpu.VMEM((3, COLUMNS, SPAN), jnp.int32),
                pltpu.VMEM((3, COLUMNS, SPAN), f32),
                pltpu.VMEM((COLUMNS, SPAN), f32),
                pltpu.VMEM((FIELDS, ROWS, SPAN), f32),
                pltpu.VMEM((3, FIELDS, ROWS, SPAN), f32),
                pltpu.VMEM((3, FIELDS, ROWS, SPAN), f32),
                pltpu.VMEM((FIELDS + 1, ROWS, SPAN), f32),
                pltpu.VMEM((FIELDS + 1, ROWS, SPAN), f32),
                pltpu.VMEM((FIELDS + 1, ROWS, SPAN), f32),
                pltpu.SemaphoreType.DMA((8,)),
                pltpu.SemaphoreType.DMA((2, chunks)),
                pltpu.SemaphoreType.DMA((2, chunks)),
                pltpu.SemaphoreType.DMA((2, 2)),
                pltpu.SemaphoreType.DMA((2, 2)),
                pltpu.SemaphoreType.DMA((8,)),
                pltpu.SemaphoreType.DMA((6,)),
            ],
            compiler_params=pltpu.CompilerParams(collective_id=0, has_side_effects=True),
        )(*args)
        return pl.pallas_call(
            functools.partial(substitute, levels),
            out_shape=[jax.ShapeDtypeStruct(args[0].shape, f32)] * FIELDS,
            in_specs=[vmem] * 2,
            out_specs=[anywhere] * FIELDS,
            scratch_shapes=[
                pltpu.VMEM((groups * LEVELS - 1, ROWS, SPAN), f32),
                pltpu.SemaphoreType.DMA((3, FIELDS)),
            ],
        )(*(pltpu.with_memory_space_constraint(q, pltpu.VMEM) for q in (y, r)))

    wide, flat = P(None, "lon", "lat"), P("lon", "lat")
    return jax.shard_map(
        shards,
        mesh=mesh,
        in_specs=(wide,) * 4 + (flat,) * 3,
        out_specs=(wide,) * 4,
        check_vma=False,
    )
```
